128 devices in a mesh: row: 8 (over x, core), col: 16 (over z, y).
Axes of the slice: x: 4, y: 4, z: 4, core: 2. Of those that a mesh axis runs over, the one named last changes fastest.
Arguments:
- panel_inverse: bfloat16 [2, 2, 2, 1024, 1024], P(None, None, None, ('row', 'col')), may hold values from -0.125 to 0.125
- panel_below: bfloat16 [2, 2, 1024, 1024], P(None, None, ('row', 'col')), may hold values from -0.5 to 0.5
- trail_factor: bfloat16 [2, 2, 2, 131072, 1024], P(None, None, None, ('row', 'col')), may hold values from -0.125 to 0.125
- first_rhs: bfloat16 [2, 2, 1024, 256], replicated, may hold values from -6 to 6
- second_rhs: bfloat16 [2, 2, 1024, 256], P(None, None, ('row', 'col')), may hold values from -6 to 6
- trail_rhs: bfloat16 [2, 2, 131072, 256], P(None, None, ('row', 'col')), may hold values from -6 to 6
- shape_tiles: float32 [2, 9, 2, 1024], P(None, None, None, ('row', 'col')), may hold values from -0.25 to 0.25
- element_vertices: int32 [2, 1024, 3], P(None, ('row', 'col')), may hold values from 0 to 1023, all different within a row
- vertex_slot: int32 [1024], replicated, may hold values from 0 to 1023, each once
Outputs:
- panel_solution: bfloat16 [2, 2, 2, 1024, 256], P(None, None, None, ('row', 'col'))
- trail_update: bfloat16 [2, 2, 131072, 256], P(None, None, ('row', 'col'))
- vertex_gradient: float32 [3, 1024], P(None, ('row', 'col'))
The draws below stay inside these ranges and needn't reach their ends.
Inputs may be any that keep to these rules, and one draw needn't show every extreme that they name: `element_vertices`: each element names three different vertices, and every vertex is named by some element. `vertex_slot`: each slot is given to exactly one vertex.
All inputs are finite; a program needn't handle non-finite values.
Results may differ from the reference program's by a relative error of at most 0.0067.
Values may be sent and summed in bfloat16 or wider, within the bound.
No kernel may reach another device: no remote copies, remote signals or barrier semaphores. Data moves between devices by JAX's collectives and lax.ppermute only.
A program may use at most 128 MiB of HBM per device.

```python
import jax
import jax.numpy as jnp
from jax import lax

NB = 1024
ANG = 256
ORDER = 131072
NV = 1024


def raised(drawn, stream_key, source, target, blocks, factor):
    owner, partner = [(jnp.arange(drawn.shape[position]) // (drawn.shape[position] // blocks)).reshape([-1 if axis == position else 1 for axis in range(drawn.ndim)]) for position in (source, target)]
    chosen = jax.random.permutation(stream_key, blocks)[partner]
    strong = (owner == chosen) | (owner == (partner + blocks // 2) % blocks)
    return jnp.where(strong, factor * drawn, drawn)


def block_levels(rng, extent, pieces, smallest, high):
    def one(axis_at, parts):
        draws = jax.random.uniform(jax.random.fold_in(jax.random.fold_in(rng, 6), axis_at), (parts,), jnp.float32, smallest / len(pieces), high / len(pieces))
        return jnp.repeat(jnp.exp(draws), extent[axis_at] // parts).reshape((-1,) + (1,) * (len(extent) - axis_at - 1))

    loudness = one(*pieces[0])
    for cut in pieces[1:]:
        loudness = loudness * one(*cut)
    return loudness


def picks_of(key, rows, number_of, top, lift):
    ranking = jax.random.permutation(jax.random.fold_in(key, 1), number_of)
    boost = ranking
    for power in range(3):
        boost = boost * boost // number_of
    boost = boost * lift // number_of
    lots = jax.random.randint(jax.random.fold_in(key, 2), (rows, number_of), 0, 4096) + boost
    fixed_rows = jax.random.permutation(jax.random.fold_in(key, 3), rows)[jnp.arange(number_of) % rows]
    lots = jnp.where(jnp.arange(rows)[:, None] == fixed_rows[None, :], 1 << 14, lots)
    merit = lots * number_of + jnp.arange(number_of)
    return lax.top_k(merit.astype(jnp.int32), top)[1].astype(jnp.int32)


def bell_draw(own_key, shape, spread, bound, shards=(), kind=jnp.bfloat16):
    loudness = block_levels(own_key, shape, shards, -0.22, 0.18) if shards else 1.0
    entries = jax.random.normal(own_key, shape, jnp.float32) * spread * loudness
    return jnp.minimum(jnp.maximum(entries, -bound), bound).astype(kind)


def noise_with(key, shape, width, bound, shards, heavy, dtype=jnp.bfloat16):
    drawn = width * jax.random.normal(key, shape, jnp.float32)
    if shards:
        drawn = drawn * block_levels(key, shape, shards, -0.22, 0.18)
    return jnp.clip(raised(drawn, jax.random.fold_in(key, 3), *heavy), -bound, bound).astype(dtype)


def setup_inputs(seed: int = 0) -> dict:
    key_list = jax.random.split(jax.random.key(seed), 10)
    panel_inverse = bell_draw(key_list[0], (2, 2, 2, NB, NB), (2 * NB) ** -0.5, 0.125, ((3, 128),))
    panel_below = noise_with(key_list[1], (2, 2, NB, NB), (2 * NB) ** -0.5, 0.5, ((2, 128),), (2, 3, 128, 5.5))
    trail_factor = bell_draw(key_list[2], (2, 2, 2, ORDER, NB), (2 * NB) ** -0.5, 0.125, ((3, 128),))
    first_rhs = bell_draw(key_list[3], (2, 2, NB, ANG), 1.0, 6.0)
    second_rhs = bell_draw(key_list[4], (2, 2, NB, ANG), 1.0, 6.0, ((2, 128),))
    trail_rhs = bell_draw(key_list[5], (2, 2, ORDER, ANG), 1.0, 6.0, ((2, 128),))
    shape_tiles = bell_draw(key_list[6], (2, 9, 2, NB), (0.25 * ANG ** -0.5), 0.25, ((3, 128),), jnp.float32)
    element_vertices = picks_of(key_list[7], 2 * NB, NV, 3, 48).reshape((2, NB, 3))
    vertex_slot = jax.random.permutation(key_list[8], NV).astype(jnp.int32)
    return dict(panel_inverse=panel_inverse, panel_below=panel_below, trail_factor=trail_factor, first_rhs=first_rhs, second_rhs=second_rhs, trail_rhs=trail_rhs, shape_tiles=shape_tiles, element_vertices=element_vertices, vertex_slot=vertex_slot)


def complex_dot(left_real, left_imag, right_real, right_imag):
    left_real = left_real.astype(jnp.float32)
    left_imag = left_imag.astype(jnp.float32)
    right_real = right_real.astype(jnp.float32)
    right_imag = right_imag.astype(jnp.float32)
    real_part = jnp.dot(left_real, right_real, preferred_element_type=jnp.float32) - jnp.dot(left_imag, right_imag, preferred_element_type=jnp.float32)
    imag_part = jnp.dot(left_real, right_imag, preferred_element_type=jnp.float32) + jnp.dot(left_imag, right_real, preferred_element_type=jnp.float32)
    return real_part, imag_part


def couple_partials(panel_solution, shape_tiles):
    forward = panel_solution[0].astype(jnp.float32)
    adjoint = panel_solution[1].astype(jnp.float32)
    coupling_real = jnp.sum(forward[:, 0] * adjoint[:, 0] - forward[:, 1] * adjoint[:, 1], axis=-1)
    coupling_imag = jnp.sum(forward[:, 0] * adjoint[:, 1] + forward[:, 1] * adjoint[:, 0], axis=-1)
    return -(shape_tiles[0] * coupling_real - shape_tiles[1] * coupling_imag)


def spread_vertices(partials, element_vertices, vertex_slot, vertex_count):
    values = jnp.transpose(partials.reshape(3, 3, partials.shape[1], partials.shape[2]), (1, 2, 3, 0))
    slots = vertex_slot[element_vertices].astype(jnp.int32)
    empty = jnp.zeros((3, vertex_count), jnp.float32)
    return empty.at[:, slots.reshape(-1)].add(values.reshape(3, -1))


def reference(panel_inverse, panel_below, trail_factor, first_rhs, second_rhs, trail_rhs, shape_tiles, element_vertices, vertex_slot):
    solutions = []
    updates = []
    for system in range(2):
        inverse = panel_inverse[system]
        first_real, first_imag = complex_dot(inverse[0, 0], inverse[0, 1], first_rhs[system, 0], first_rhs[system, 1])
        first_real = first_real.astype(jnp.bfloat16)
        first_imag = first_imag.astype(jnp.bfloat16)
        below_real, below_imag = complex_dot(panel_below[system, 0].T, panel_below[system, 1].T, first_real, first_imag)
        right_real = (second_rhs[system, 0].astype(jnp.float32) - below_real).astype(jnp.bfloat16)
        right_imag = (second_rhs[system, 1].astype(jnp.float32) - below_imag).astype(jnp.bfloat16)
        second_real, second_imag = complex_dot(inverse[1, 0], inverse[1, 1], right_real, right_imag)
        second_real = second_real.astype(jnp.bfloat16)
        second_imag = second_imag.astype(jnp.bfloat16)
        update_real = trail_rhs[system, 0].astype(jnp.float32)
        update_imag = trail_rhs[system, 1].astype(jnp.float32)
        pairs = ((first_real, first_imag), (second_real, second_imag))
        for section_index in range(2):
            term_real, term_imag = complex_dot(trail_factor[system, section_index, 0], trail_factor[system, section_index, 1], pairs[section_index][0], pairs[section_index][1])
            update_real = update_real - term_real
            update_imag = update_imag - term_imag
        updates.append(jnp.stack([update_real, update_imag]).astype(jnp.bfloat16))
        solutions.append(jnp.stack([jnp.stack([first_real, first_imag]), jnp.stack([second_real, second_imag])]))
    panel_solution = jnp.stack(solutions)
    trail_update = jnp.stack(updates)
    partials = couple_partials(panel_solution, shape_tiles)
    vertex_gradient = spread_vertices(partials, element_vertices, vertex_slot, NV)
    return panel_solution, trail_update, vertex_gradient
```

```python
import jax
import jax.numpy as jnp
from jax import lax
from jax.sharding import Mesh
from jax.sharding import PartitionSpec as P

ALL = ("x", "core", "col")
F32 = jnp.float32
BF16 = jnp.bfloat16


def complex_pair(left_real, left_imag, right):
    stacked = jnp.concatenate([left_real, left_imag], axis=0)
    product = jnp.dot(stacked, right, preferred_element_type=F32)
    return fold_parts(product)


def fold_parts(product):
    half = product.shape[0] // 2
    top, low = product[:half], product[half:]
    return jnp.concatenate([top[:, :64] - low[:, 64:], top[:, 64:] + low[:, :64]], axis=1)


def complex_rows(left, right):
    form = "prn,qna->pqra"
    product = jnp.einsum(form, left, right, preferred_element_type=F32)
    return jnp.stack([product[0, 0] - product[1, 1], product[0, 1] + product[1, 0]])


def gather_x(value, x):
    rounds = [value]
    for step in range(1, 4):
        rounds.append(lax.ppermute(value, "x", [(i, (i + step) % 4) for i in range(4)]))
    stacked = jnp.stack(rounds)
    return jnp.stack([lax.dynamic_index_in_dim(stacked, (x - i) % 4, 0, keepdims=False) for i in range(4)])


def swap_core(value):
    return lax.ppermute(value, "core", [(0, 1), (1, 0)])


def element_tile(shape_tiles, element_vertices, vertex_slot):
    values = shape_tiles.transpose(3, 0, 2, 1).reshape(8, 36)
    high = lax.reduce_precision(values, 8, 7)
    rest = values - high
    mid = lax.reduce_precision(rest, 8, 7)
    low = rest - mid
    slots = vertex_slot[element_vertices].transpose(1, 0, 2).reshape(8, 6)
    parts = [high, mid, low, (slots // 32).astype(F32), (slots % 32).astype(F32), jnp.zeros((8, 8), F32)]
    return jnp.concatenate(parts, axis=1).astype(BF16)


def body(
    panel_inverse,
    panel_below,
    trail_factor,
    first_rhs,
    second_rhs,
    trail_rhs,
    shape_tiles,
    element_vertices,
    vertex_slot,
):
    x = lax.axis_index("x")
    core = lax.axis_index("core")
    device = lax.axis_index(ALL)
    tile = element_tile(shape_tiles, element_vertices, vertex_slot)

    first = jnp.stack(
        [complex_rows(panel_inverse[s, 0], first_rhs[s]) for s in range(2)]
    ).astype(BF16)
    send_first = first.reshape(2, 2, 8, 4, 64).transpose(3, 0, 2, 1, 4).reshape(4, 2, 1, 8, 128)
    send_below = (
        panel_below.reshape(2, 2, 8, 8, 16, 8).transpose(0, 4, 2, 1, 3, 5).reshape(1, 2, 16, 8, 128)
    )
    full = (4, 2, 16, 8, 128)
    send = jnp.stack([jnp.broadcast_to(send_first, full), jnp.broadcast_to(send_below, full)], axis=3)
    received = lax.all_to_all(send.reshape(128, 2, 8, 128), ALL, 0, 0, tiled=True)
    first_block = received[:, 0].reshape(1024, 128)
    below_block = received[:, 1].reshape(1024, 128)

    pack = jnp.concatenate([panel_inverse[:, 1], second_rhs], axis=-1)
    own = lax.dynamic_index_in_dim(pack, core, 0, keepdims=False)
    other = swap_core(lax.dynamic_index_in_dim(pack, 1 - core, 0, keepdims=False))
    chip = jnp.where(core == 0, jnp.stack([own, other]), jnp.stack([other, own]))
    rows = gather_x(chip, x)
    rows = rows.transpose(2, 0, 1, 3, 4).reshape(2, 64, 1280)
    inverse_rows = rows[:, :, :1024]
    right_rows = lax.dynamic_slice_in_dim(rows[:, :, 1024:], 64 * x, 64, 2)
    right_rows = jnp.concatenate([right_rows[0], right_rows[1]], axis=1).astype(F32)

    product = lax.dot_general(
        below_block, first_block, (((0,), (0,)), ((), ())), preferred_element_type=F32
    )
    right = (right_rows - fold_parts(product)).astype(BF16)
    send = jnp.broadcast_to(jnp.concatenate([right, tile])[None], (16, 72, 128))
    received = lax.all_to_all(send, "col", 0, 0, tiled=True)
    right_block = received[:, :64].reshape(16, 8, 8, 128).transpose(1, 0, 2, 3).reshape(1024, 128)
    tiles = received[:, 64:].reshape(128, 128)
    second = complex_pair(inverse_rows[0], inverse_rows[1], right_block).astype(BF16)

    first_all = gather_x(jnp.concatenate([first_block, tiles]), x)
    first_other = swap_core(first_all)

    send = jnp.broadcast_to(second[None], (64, 64, 128))
    second_all = lax.all_to_all(send, ("x", "col"), 0, 0, tiled=True)
    second_all = (
        second_all.reshape(4, 16, 8, 8, 128).transpose(0, 2, 1, 3, 4).reshape(4, 1024, 128)
    )
    second_other = swap_core(second_all)

    def by_system(mine, theirs):
        pair = jnp.where(core == 0, jnp.stack([mine, theirs]), jnp.stack([theirs, mine]))
        return pair.reshape(2, 4, -1, 2, 64).transpose(0, 3, 2, 1, 4).reshape(2, 2, -1, 256)

    first_full = by_system(first_all[:, :1024], first_other[:, :1024])
    second_full = by_system(second_all, second_other)

    updates = []
    for s in range(2):
        total = trail_rhs[s].astype(F32) - complex_rows(trail_factor[s, 0], first_full[s])
        total = total - complex_rows(trail_factor[s, 1], second_full[s])
        updates.append(total)
    trail_update = jnp.stack(updates).astype(BF16)

    own_second = lax.dynamic_slice_in_dim(second_full, 8 * device, 8, 2)
    panel_solution = jnp.stack([first, own_second], axis=1)

    tiles_pair = jnp.stack([first_all[:, 1024:], first_other[:, 1024:]], axis=1)
    tiles_pair = jnp.where(core == 0, tiles_pair, tiles_pair[:, ::-1]).reshape(1024, 128).astype(F32)
    shapes = tiles_pair[:, :36] + tiles_pair[:, 36:72] + tiles_pair[:, 72:108]
    shapes = shapes.reshape(1024, 2, 2, 9)
    slots = 32.0 * tiles_pair[:, 108:114] + tiles_pair[:, 114:120]
    slots = slots.reshape(1024, 2, 3)
    mask = slots[..., None] == (8 * device + jnp.arange(8)).astype(F32)
    gradient = jnp.zeros((3, 8), F32)
    for t, full in enumerate((first_full, second_full)):
        forward = full[0].astype(F32)
        adjoint = full[1].astype(F32)
        real = jnp.sum(forward[0] * adjoint[0] - forward[1] * adjoint[1], axis=-1)
        imag = jnp.sum(forward[0] * adjoint[1] + forward[1] * adjoint[0], axis=-1)
        partial = -(shapes[:, 0, t] * real[:, None] - shapes[:, 1, t] * imag[:, None])
        partial = partial.reshape(1024, 3, 3)
        gradient = gradient + jnp.sum(
            jnp.where(mask[:, t, :, None, :], partial[..., None], 0.0), axis=(0, 1)
        )
    return (panel_solution, trail_update, gradient)


def solution(mesh):
    fine = Mesh(mesh.devices.reshape(4, 2, 16), ALL)
    return jax.shard_map(
        body,
        mesh=fine,
        in_specs=(
            P(None, None, None, ALL, None),
            P(None, None, ALL, None),
            P(None, None, None, ALL, None),
            P(),
            P(None, None, ALL, None),
            P(None, None, ALL, None),
            P(None, None, None, ALL),
            P(None, ALL, None),
            P(),
        ),
        out_specs=(
            P(None, None, None, ALL, None),
            P(None, None, ALL, None),
            P(None, ALL),
        ),
        check_vma=False,
    )
```

```python
import jax
import jax.numpy as jnp
import numpy as np
from jax import lax
from jax.experimental import pallas as pl
from jax.experimental.pallas import tpu as pltpu
from jax.sharding import Mesh
from jax.sharding import PartitionSpec as P

ALL = ("x", "core", "col")
F32 = jnp.float32
BF16 = jnp.bfloat16
VMEM_LIMIT = 48 * 1024 * 1024


def lanes_below(shape, bound):
    return lax.broadcasted_iota(jnp.int32, shape, len(shape) - 1) < bound


def pair_lanes(left, right):
    low = lanes_below(left.shape, 64)
    real = jnp.where(low, left, pltpu.roll(right, 64, 1))
    imag = jnp.where(low, pltpu.roll(left, 64, 1), right)
    return real, imag


def fold_parts(top, low):
    turned = pltpu.roll(low, 64, 1)
    return top + jnp.where(lanes_below(low.shape, 64), -turned, turned)


def prepare_kernel(place, inverse, rhs, below, own_rhs, first, send, own, give):
    system = pl.program_id(0)
    left = jnp.concatenate([inverse[0, 0, 0].astype(F32), inverse[0, 0, 1].astype(F32)]).astype(BF16)
    by_real = jnp.dot(left, rhs[0, 0], preferred_element_type=F32)
    by_imag = jnp.dot(left, rhs[0, 1], preferred_element_type=F32)
    real = (by_real[:8] - by_imag[8:]).astype(BF16)
    imag = (by_imag[:8] + by_real[8:]).astype(BF16)
    first[0, 0] = real
    first[0, 1] = imag
    real = real.astype(F32)
    imag = imag.astype(F32)
    for half in range(2):
        cut = slice(128 * half, 128 * half + 128)
        even, odd = pair_lanes(real[:, cut], imag[:, cut])
        for group, value in ((2 * half, even), (2 * half + 1, odd)):
            value = value.astype(BF16)
            for col in range(16):
                send[group, 0, col, 0] = value
    lane_block = lax.broadcasted_iota(jnp.int32, (8, 128), 1) // 8
    pieces = [
        below[0, part, :, 128 * row : 128 * row + 128].astype(F32)
        for part in range(2)
        for row in range(8)
    ]
    for col in range(16):
        value = pltpu.roll(pieces[0], (128 - 8 * col) % 128, 1)
        for block in range(1, 16):
            turned = pltpu.roll(pieces[block], (8 * block - 8 * col) % 128, 1)
            value = jnp.where(lane_block == block, turned, value)
        value = value.astype(BF16)
        for group in range(4):
            send[group, 0, col, 1] = value

    def fill(target):
        for part in range(2):
            target[part, :, :1024] = inverse[0, 1, part]
            target[part, :, 1024:] = own_rhs[0, part]

    @pl.when(system == place[1])
    def _():
        fill(own)

    @pl.when(system != place[1])
    def _():
        fill(give)


def prepare(place, panel_inverse, first_rhs, panel_below, second_rhs):
    return pl.pallas_call(
        prepare_kernel,
        grid_spec=pltpu.PrefetchScalarGridSpec(
            num_scalar_prefetch=1,
            grid=(2,),
            in_specs=[
                pl.BlockSpec((1, 2, 2, 8, 1024), lambda s, _: (s, 0, 0, 0, 0)),
                pl.BlockSpec((1, 2, 1024, 256), lambda s, _: (s, 0, 0, 0)),
                pl.BlockSpec((1, 2, 8, 1024), lambda s, _: (s, 0, 0, 0)),
                pl.BlockSpec((1, 2, 8, 256), lambda s, _: (s, 0, 0, 0)),
            ],
            out_specs=[
                pl.BlockSpec((1, 2, 8, 256), lambda s, _: (s, 0, 0, 0)),
                pl.BlockSpec((4, 1, 16, 2, 8, 128), lambda s, _: (0, s, 0, 0, 0, 0)),
                pl.BlockSpec((2, 8, 1280), lambda s, _: (0, 0, 0)),
                pl.BlockSpec((2, 8, 1280), lambda s, _: (0, 0, 0)),
            ],
        ),
        out_shape=[
            jax.ShapeDtypeStruct((2, 2, 8, 256), BF16),
            jax.ShapeDtypeStruct((4, 2, 16, 2, 8, 128), BF16),
            jax.ShapeDtypeStruct((2, 8, 1280), BF16),
            jax.ShapeDtypeStruct((2, 8, 1280), BF16),
        ],
        name="prepare",
    )(place, panel_inverse, first_rhs, panel_below, second_rhs)


def right_kernel(place, received, rows0, rows1, rows2, rows3, tile, block, send, offset):
    x = place[0]
    half = pl.multiple_of(1024 + 128 * (x // 2), 128)
    odd = x % 2 == 1
    for step, rows in enumerate((rows0, rows1, rows2, rows3)):
        source = lax.rem(x - step + 4, 4)
        for core in range(2):
            real = rows[core, 0, :, pl.ds(half, 128)].astype(F32)
            imag = rows[core, 1, :, pl.ds(half, 128)].astype(F32)
            even_pair, odd_pair = pair_lanes(real, imag)
            value = jnp.where(odd, odd_pair, even_pair)
            offset[pl.ds(pl.multiple_of(16 * source + 8 * core, 8), 8), :] = value
    first = received[:, 0].astype(F32).reshape(1024, 128).astype(BF16)
    below = received[:, 1].astype(F32).reshape(1024, 128).astype(BF16)
    block[...] = first
    product = lax.dot_general(below, first, (((0,), (0,)), ((), ())), preferred_element_type=F32)
    right = (offset[...] - fold_parts(product[:64], product[64:])).astype(BF16)
    for col in range(16):
        send[col, :64] = right
        send[col, 64:] = tile[...]


def right_side(place, received, rows, tile):
    return pl.pallas_call(
        right_kernel,
        grid_spec=pltpu.PrefetchScalarGridSpec(
            num_scalar_prefetch=1,
            grid=(1,),
            in_specs=[pl.BlockSpec((128, 2, 8, 128), lambda i, _: (0, 0, 0, 0))]
            + [pl.BlockSpec((2, 2, 8, 1280), lambda i, _: (0, 0, 0, 0))] * 4
            + [pl.BlockSpec((8, 128), lambda i, _: (0, 0))],
            out_specs=[
                pl.BlockSpec((1024, 128), lambda i, _: (0, 0)),
                pl.BlockSpec((16, 72, 128), lambda i, _: (0, 0, 0)),
            ],
            scratch_shapes=[pltpu.VMEM((64, 128), F32)],
        ),
        out_shape=[
            jax.ShapeDtypeStruct((1024, 128), BF16),
            jax.ShapeDtypeStruct((16, 72, 128), BF16),
        ],
        name="right_side",
    )(place, received, *rows, tile)


def second_kernel(place, received, rows0, rows1, rows2, rows3, tiles, send):
    x = place[0]
    right = received[:, :64].astype(F32).reshape(16, 8, 8, 128)
    right = right.transpose(1, 0, 2, 3).reshape(1024, 128).astype(BF16)
    pieces = [
        rows[core, part, :, :1024].astype(F32)
        for part in range(2)
        for rows in (rows0, rows1, rows2, rows3)
        for core in range(2)
    ]
    left = jnp.concatenate(pieces).astype(BF16)
    product = jnp.dot(left, right, preferred_element_type=F32)
    value = fold_parts(product[:64], product[64:]).astype(BF16)
    for step in range(4):
        target = pl.multiple_of(16 * lax.rem(x - step + 4, 4), 16)
        part = value[16 * step : 16 * step + 16]
        for copy in range(64):
            send[copy, pl.ds(target, 16), :] = part
    tiles[...] = received[:, 64:].astype(F32).reshape(128, 128).astype(BF16)


def second_rows(place, received, rows):
    return pl.pallas_call(
        second_kernel,
        grid_spec=pltpu.PrefetchScalarGridSpec(
            num_scalar_prefetch=1,
            grid=(1,),
            in_specs=[pl.BlockSpec((16, 72, 128), lambda i, _: (0, 0, 0))]
            + [pl.BlockSpec((2, 2, 8, 1280), lambda i, _: (0, 0, 0, 0))] * 4,
            out_specs=[
                pl.BlockSpec((128, 128), lambda i, _: (0, 0)),
                pl.BlockSpec((64, 64, 128), lambda i, _: (0, 0, 0)),
            ],
        ),
        out_shape=[
            jax.ShapeDtypeStruct((128, 128), BF16),
            jax.ShapeDtypeStruct((64, 64, 128), BF16),
        ],
        name="second_rows",
    )(place, received, *rows)


def store_weights(weights, at, real_pairs):
    for half, (left, right) in enumerate(real_pairs):
        real, imag = pair_lanes(left, right)
        lane = 128 * half
        weights[pl.ds(at, 128), lane : lane + 128] = real.astype(BF16)
        weights[pl.ds(at, 128), 256 + lane : 384 + lane] = imag.astype(BF16)
        weights[pl.ds(at + 1024, 128), lane : lane + 128] = (-imag).astype(BF16)
        weights[pl.ds(at + 1024, 128), 256 + lane : 384 + lane] = real.astype(BF16)


def trail_product(factor, weights):
    total = jnp.dot(factor[0, 0, 0], weights[:1024], preferred_element_type=F32)
    return total + jnp.dot(factor[0, 0, 1], weights[1024:], preferred_element_type=F32)


def trail_first_kernel(place, b0, b1, b2, b3, c0, c1, c2, c3, factor, rhs, out, ordered, weights):
    x = place[0]
    turn = pl.program_id(0)

    def build(blocks):
        for step, block in enumerate(blocks):
            ordered[lax.rem(x - step + 4, 4)] = block[...]

        def chunk(row, carry):
            at = pl.multiple_of(128 * row, 128)
            parts = [ordered[q, pl.ds(at, 128), :].astype(F32) for q in range(4)]
            store_weights(weights, at, ((parts[0], parts[1]), (parts[2], parts[3])))
            return carry

        lax.fori_loop(0, 8, chunk, 0)

    @pl.when((turn == 0) & (pl.program_id(1) == 0))
    def _():
        build((b0, b1, b2, b3))

    @pl.when((turn == 1) & (pl.program_id(1) == 0))
    def _():
        build((c0, c1, c2, c3))

    total = trail_product(factor, weights)
    out[0, 0] = rhs[0, 0].astype(F32) - total[:, :256]
    out[0, 1] = rhs[0, 1].astype(F32) - total[:, 256:]


def trail_first(place, blocks, trail_factor, trail_rhs):
    rows = trail_rhs.shape[2]
    height = min(256, rows)
    system = lambda turn, p: jnp.where(turn == 0, p[1], 1 - p[1])
    return pl.pallas_call(
        trail_first_kernel,
        grid_spec=pltpu.PrefetchScalarGridSpec(
            num_scalar_prefetch=1,
            grid=(2, rows // height),
            in_specs=[pl.BlockSpec((1024, 128), lambda t, i, p: (0, 0))] * 8
            + [
                pl.BlockSpec((1, 1, 2, height, 1024), lambda t, i, p: (system(t, p), 0, 0, i, 0)),
                pl.BlockSpec((1, 2, height, 256), lambda t, i, p: (system(t, p), 0, i, 0)),
            ],
            out_specs=pl.BlockSpec((1, 2, height, 256), lambda t, i, p: (system(t, p), 0, i, 0)),
            scratch_shapes=[pltpu.VMEM((4, 1024, 128), BF16), pltpu.VMEM((2048, 512), BF16)],
        ),
        out_shape=jax.ShapeDtypeStruct((2, 2, rows, 256), F32),
        compiler_params=pltpu.CompilerParams(vmem_limit_bytes=VMEM_LIMIT),
        name="trail_first",
    )(place, *blocks, trail_factor, trail_rhs)


def trail_second_kernel(place, blocks, factor, partial, *refs):
    out, own, weights = refs[-3:]

    @pl.when(pl.program_id(0) == 0)
    def _():
        def chunk(row, carry):
            at = pl.multiple_of(128 * row, 128)
            near = pl.multiple_of(8 * row, 8)
            parts = [
                blocks[q, :, pl.ds(near, 8), :].astype(F32).reshape(128, 128) for q in range(4)
            ]
            store_weights(weights, at, ((parts[0], parts[1]), (parts[2], parts[3])))
            return carry

        lax.fori_loop(0, 8, chunk, 0)
        near = pl.multiple_of(8 * place[3], 8)
        parts = [blocks[q, place[4], pl.ds(near, 8), :].astype(F32) for q in range(4)]
        for half in range(2):
            real, imag = pair_lanes(parts[2 * half], parts[2 * half + 1])
            own[0, :, 128 * half : 128 * half + 128] = real.astype(BF16)
            own[1, :, 128 * half : 128 * half + 128] = imag.astype(BF16)

    total = trail_product(factor, weights)
    out[0, 0] = (partial[0, 0] - total[:, :256]).astype(BF16)
    out[0, 1] = (partial[0, 1] - total[:, 256:]).astype(BF16)


def trail_second(place, which, blocks, trail_factor, partial, previous=None):
    rows = partial.shape[2]
    height = min(256, rows)
    place = jnp.concatenate([place[:2], which[None], place[2:]])
    extra = () if previous is None else (previous,)
    return pl.pallas_call(
        trail_second_kernel,
        grid_spec=pltpu.PrefetchScalarGridSpec(
            num_scalar_prefetch=1,
            grid=(rows // height,),
            in_specs=[
                pl.BlockSpec((4, 16, 64, 128), lambda i, p: (0, 0, 0, 0)),
                pl.BlockSpec((1, 1, 2, height, 1024), lambda i, p: (p[2], 1, 0, i, 0)),
                pl.BlockSpec((1, 2, height, 256), lambda i, p: (p[2], 0, i, 0)),
            ]
            + [pl.BlockSpec(memory_space=pl.ANY)] * len(extra),
            out_specs=[
                pl.BlockSpec((1, 2, height, 256), lambda i, p: (p[2], 0, i, 0)),
                pl.BlockSpec((2, 8, 256), lambda i, p: (0, 0, 0)),
            ],
            scratch_shapes=[pltpu.VMEM((2048, 512), BF16)],
        ),
        out_shape=[
            jax.ShapeDtypeStruct((2, 2, rows, 256), BF16),
            jax.ShapeDtypeStruct((2, 8, 256), BF16),
        ],
        input_output_aliases={4: 0} if extra else {},
        compiler_params=pltpu.CompilerParams(vmem_limit_bytes=VMEM_LIMIT),
        name="trail_second",
    )(place, blocks, trail_factor, partial, *extra)


def spread_matrix(panel):
    spread = np.zeros((128, 3, 128), np.float32)
    for corner in range(3):
        for coordinate in range(3):
            lanes = slice(24 * corner + 8 * coordinate, 24 * corner + 8 * coordinate + 8)
            for part in range(2):
                source = 18 * part + 9 * panel + 3 * corner + coordinate
                for term in range(3):
                    spread[36 * term + source, part, lanes] = 1.0
            spread[108 + 3 * panel + corner, 2, lanes] = 32.0
            spread[114 + 3 * panel + corner, 2, lanes] = 1.0
    return jnp.asarray(spread.reshape(128, 384), BF16)


def gradient_sum(place, couple, tile_refs, spread, chunk_of):
    base = 8 * (16 * place[2] + place[3])
    target = (base + lax.rem(lax.broadcasted_iota(jnp.int32, (128, 128), 1), 8)).astype(F32)
    sign = jnp.where(lanes_below((128, 128), 64), 1.0, -1.0)
    total = jnp.zeros((8, 128), F32)
    for step in range(4):
        source = lax.rem(place[0] - step + 4, 4)
        for side in range(2):
            core = place[1] if side == 0 else 1 - place[1]
            same, crossed = couple(2 * source + core)
            real = jnp.sum(same * sign, axis=1, keepdims=True)
            imag = jnp.sum(crossed, axis=1, keepdims=True)
            table = jnp.dot(tile_refs[4 * side + step][...], spread[...], preferred_element_type=F32)
            value = table[:, 128:256] * imag - table[:, :128] * real
            value = jnp.where(table[:, 256:] == target, value, 0.0)
            total = total + jnp.sum(value.reshape(16, 8, 128), axis=0)
    return total


def couple_pairs(pairs):
    same = jnp.zeros((128, 128), F32)
    crossed = jnp.zeros((128, 128), F32)
    for mine, theirs in pairs:
        same = same + mine * theirs
        crossed = crossed + mine * pltpu.roll(theirs, 64, 1)
    return same, crossed


def gradient_first_kernel(place, *refs):
    blocks, tiles, spread, out = refs[:8], refs[8:16], refs[16], refs[17]

    def couple(row):
        at = pl.multiple_of(128 * row, 128)
        return couple_pairs(
            (blocks[q][pl.ds(at, 128), :].astype(F32), blocks[4 + q][pl.ds(at, 128), :].astype(F32))
            for q in range(4)
        )

    out[...] = gradient_sum(place, couple, tiles, spread, None)


def gradient_first(place, blocks, tiles, spread):
    return pl.pallas_call(
        gradient_first_kernel,
        grid_spec=pltpu.PrefetchScalarGridSpec(
            num_scalar_prefetch=1,
            grid=(1,),
            in_specs=[pl.BlockSpec((1024, 128), lambda i, p: (0, 0))] * 8
            + [pl.BlockSpec((128, 128), lambda i, p: (0, 0))] * 8
            + [pl.BlockSpec((128, 384), lambda i, p: (0, 0))],
            out_specs=pl.BlockSpec((8, 128), lambda i, p: (0, 0)),
        ),
        out_shape=jax.ShapeDtypeStruct((8, 128), F32),
        compiler_params=pltpu.CompilerParams(vmem_limit_bytes=VMEM_LIMIT),
        name="gradient_first",
    )(place, *blocks, *tiles, spread)


def gradient_second_kernel(place, mine, theirs, *refs):
    tiles, spread, before, out = refs[:8], refs[8], refs[9], refs[10]

    def couple(row):
        near = pl.multiple_of(8 * row, 8)
        return couple_pairs(
            (
                mine[q, :, pl.ds(near, 8), :].astype(F32).reshape(128, 128),
                theirs[q, :, pl.ds(near, 8), :].astype(F32).reshape(128, 128),
            )
            for q in range(4)
        )

    total = before[...] + gradient_sum(place, couple, tiles, spread, None)
    total = jnp.sum(total, axis=0, keepdims=True)
    total = total + pltpu.roll(total, 104, 1) + pltpu.roll(total, 80, 1)
    for coordinate in range(3):
        out[coordinate : coordinate + 1, :] = total[:, 8 * coordinate : 8 * coordinate + 8]


def gradient_second(place, mine, theirs, tiles, spread, before):
    return pl.pallas_call(
        gradient_second_kernel,
        grid_spec=pltpu.PrefetchScalarGridSpec(
            num_scalar_prefetch=1,
            grid=(1,),
            in_specs=[pl.BlockSpec((4, 16, 64, 128), lambda i, p: (0, 0, 0, 0))] * 2
            + [pl.BlockSpec((128, 128), lambda i, p: (0, 0))] * 8
            + [
                pl.BlockSpec((128, 384), lambda i, p: (0, 0)),
                pl.BlockSpec((8, 128), lambda i, p: (0, 0)),
            ],
            out_specs=pl.BlockSpec((3, 8), lambda i, p: (0, 0)),
        ),
        out_shape=jax.ShapeDtypeStruct((3, 8), F32),
        compiler_params=pltpu.CompilerParams(vmem_limit_bytes=VMEM_LIMIT),
        name="gradient_second",
    )(place, mine, theirs, *tiles, spread, before)


def rounds_x(value):
    sent = [lax.ppermute(value, "x", [(i, (i + step) % 4) for i in range(4)]) for step in (1, 2, 3)]
    return [value, *sent]


def swap_core(value):
    return lax.ppermute(value, "core", [(0, 1), (1, 0)])


def element_tile(shape_tiles, element_vertices, vertex_slot):
    values = shape_tiles.transpose(3, 0, 2, 1).reshape(8, 36)
    high = lax.reduce_precision(values, 8, 7)
    rest = values - high
    mid = lax.reduce_precision(rest, 8, 7)
    low = rest - mid
    slots = vertex_slot[element_vertices].transpose(1, 0, 2).reshape(8, 6)
    parts = [high, mid, low, (slots // 32).astype(F32), (slots % 32).astype(F32), jnp.zeros((8, 8), F32)]
    return jnp.concatenate(parts, axis=1).astype(BF16)


def body(
    panel_inverse,
    panel_below,
    trail_factor,
    first_rhs,
    second_rhs,
    trail_rhs,
    shape_tiles,
    element_vertices,
    vertex_slot,
):
    x = lax.axis_index("x")
    core = lax.axis_index("core")
    col = lax.axis_index("col")
    place = jnp.stack([x, core, 2 * x + core, col]).astype(jnp.int32)

    first, send, own, give = prepare(place, panel_inverse, first_rhs, panel_below, second_rhs)
    received = lax.all_to_all(send.reshape(128, 2, 8, 128), ALL, 0, 0, tiled=True)

    other = swap_core(give)
    chip = jnp.where(core == 0, jnp.stack([own, other]), jnp.stack([other, own]))
    rows = rounds_x(chip)
    tile = element_tile(shape_tiles, element_vertices, vertex_slot)

    first_block, send = right_side(place, received, rows, tile)
    received = lax.all_to_all(send, "col", 0, 0, tiled=True)
    first_mine = rounds_x(first_block)
    first_theirs = [swap_core(block) for block in first_mine]

    tiles, send = second_rows(place, received, rows)
    second_mine = lax.all_to_all(send, ("x", "col"), 0, 0, tiled=True)

    tiles_mine = rounds_x(tiles)
    tiles_all = tiles_mine + [swap_core(block) for block in tiles_mine]
    partial = trail_first(place, first_mine + first_theirs, trail_factor, trail_rhs)
    gradient = gradient_first(place, first_mine + first_theirs, tiles_all, spread_matrix(0))

    second_theirs = swap_core(second_mine)
    mine = second_mine.reshape(4, 16, 64, 128)
    theirs = second_theirs.reshape(4, 16, 64, 128)
    update, own_mine = trail_second(place, core, mine, trail_factor, partial)
    update, own_theirs = trail_second(place, 1 - core, theirs, trail_factor, partial, update)
    gradient = gradient_second(place, mine, theirs, tiles_all, spread_matrix(1), gradient)

    second = jnp.where(
        core == 0, jnp.stack([own_mine, own_theirs]), jnp.stack([own_theirs, own_mine])
    )
    return (jnp.stack([first, second], axis=1), update, gradient)


def solution(mesh):
    fine = Mesh(mesh.devices.reshape(4, 2, 16), ALL)
    return jax.shard_map(
        body,
        mesh=fine,
        in_specs=(
            P(None, None, None, ALL, None),
            P(None, None, ALL, None),
            P(None, None, None, ALL, None),
            P(),
            P(None, None, ALL, None),
            P(None, None, ALL, None),
            P(None, None, None, ALL),
            P(None, ALL, None),
            P(),
        ),
        out_specs=(
            P(None, None, None, ALL, None),
            P(None, None, ALL, None),
            P(None, ALL),
        ),
        check_vma=False,
    )
```

```python
import jax
import jax.numpy as jnp
import numpy as np
from jax import lax
from jax.experimental import pallas as pl
from jax.experimental.pallas import tpu as pltpu
from jax.sharding import Mesh
from jax.sharding import PartitionSpec as P


ALL = ("x", "core", "col")
F32 = jnp.float32
BF16 = jnp.bfloat16
VMEM_LIMIT = 48 * 1024 * 1024


def lanes_below(shape, bound):
    return lax.broadcasted_iota(jnp.int32, shape, len(shape) - 1) < bound


def pair_lanes(left, right):
    low = lanes_below(left.shape, 64)
    real = jnp.where(low, left, pltpu.roll(right, 64, 1))
    imag = jnp.where(low, pltpu.roll(left, 64, 1), right)
    return real, imag


def fold_parts(top, low):
    turned = pltpu.roll(low, 64, 1)
    return top + jnp.where(lanes_below(low.shape, 64), -turned, turned)


def prepare_kernel(place, inverse, rhs, below, own_rhs, first, send, own, give):
    system = pl.program_id(0)
    left = jnp.concatenate([inverse[0, 0, 0].astype(F32), inverse[0, 0, 1].astype(F32)]).astype(BF16)
    by_real = jnp.dot(left, rhs[0, 0], preferred_element_type=F32)
    by_imag = jnp.dot(left, rhs[0, 1], preferred_element_type=F32)
    real = (by_real[:8] - by_imag[8:]).astype(BF16)
    imag = (by_imag[:8] + by_real[8:]).astype(BF16)
    first[0, 0] = real
    first[0, 1] = imag
    real = real.astype(F32)
    imag = imag.astype(F32)
    for half in range(2):
        cut = slice(128 * half, 128 * half + 128)
        even, odd = pair_lanes(real[:, cut], imag[:, cut])
        for group, value in ((2 * half, even), (2 * half + 1, odd)):
            value = value.astype(BF16)
            for col in range(16):
                send[group, 0, col, 0] = value
    lane_block = lax.broadcasted_iota(jnp.int32, (8, 128), 1) // 8
    pieces = [
        below[0, part, :, 128 * row : 128 * row + 128].astype(F32)
        for part in range(2)
        for row in range(8)
    ]
    for col in range(16):
        value = pltpu.roll(pieces[0], (128 - 8 * col) % 128, 1)
        for block in range(1, 16):
            turned = pltpu.roll(pieces[block], (8 * block - 8 * col) % 128, 1)
            value = jnp.where(lane_block == block, turned, value)
        value = value.astype(BF16)
        for group in range(4):
            send[group, 0, col, 1] = value

    def fill(target):
        for part in range(2):
            target[part, :, :1024] = inverse[0, 1, part]
            target[part, :, 1024:] = own_rhs[0, part]

    @pl.when(system == place[1])
    def _():
        fill(own)

    @pl.when(system != place[1])
    def _():
        fill(give)


def prepare(place, panel_inverse, first_rhs, panel_below, second_rhs):
    return pl.pallas_call(
        prepare_kernel,
        grid_spec=pltpu.PrefetchScalarGridSpec(
            num_scalar_prefetch=1,
            grid=(2,),
            in_specs=[
                pl.BlockSpec((1, 2, 2, 8, 1024), lambda s, _: (s, 0, 0, 0, 0)),
                pl.BlockSpec((1, 2, 1024, 256), lambda s, _: (s, 0, 0, 0)),
                pl.BlockSpec((1, 2, 8, 1024), lambda s, _: (s, 0, 0, 0)),
                pl.BlockSpec((1, 2, 8, 256), lambda s, _: (s, 0, 0, 0)),
            ],
            out_specs=[
                pl.BlockSpec((1, 2, 8, 256), lambda s, _: (s, 0, 0, 0)),
                pl.BlockSpec((4, 1, 16, 2, 8, 128), lambda s, _: (0, s, 0, 0, 0, 0)),
                pl.BlockSpec((2, 8, 1280), lambda s, _: (0, 0, 0)),
                pl.BlockSpec((2, 8, 1280), lambda s, _: (0, 0, 0)),
            ],
        ),
        out_shape=[
            jax.ShapeDtypeStruct((2, 2, 8, 256), BF16),
            jax.ShapeDtypeStruct((4, 2, 16, 2, 8, 128), BF16),
            jax.ShapeDtypeStruct((2, 8, 1280), BF16),
            jax.ShapeDtypeStruct((2, 8, 1280), BF16),
        ],
        name="prepare",
    )(place, panel_inverse, first_rhs, panel_below, second_rhs)


def right_kernel(place, received, rows0, rows1, rows2, rows3, tile, block, send, offset):
    x = place[0]
    half = pl.multiple_of(1024 + 128 * (x // 2), 128)
    odd = x % 2 == 1
    for step, rows in enumerate((rows0, rows1, rows2, rows3)):
        source = lax.rem(x - step + 4, 4)
        for core in range(2):
            real = rows[core, 0, :, pl.ds(half, 128)].astype(F32)
            imag = rows[core, 1, :, pl.ds(half, 128)].astype(F32)
            even_pair, odd_pair = pair_lanes(real, imag)
            value = jnp.where(odd, odd_pair, even_pair)
            offset[pl.ds(pl.multiple_of(16 * source + 8 * core, 8), 8), :] = value
    first = received[:, 0].astype(F32).reshape(1024, 128).astype(BF16)
    below = received[:, 1].astype(F32).reshape(1024, 128).astype(BF16)
    block[...] = first
    product = lax.dot_general(below, first, (((0,), (0,)), ((), ())), preferred_element_type=F32)
    right = (offset[...] - fold_parts(product[:64], product[64:])).astype(BF16)
    for col in range(16):
        send[col, :64] = right
        send[col, 64:] = tile[...]


def right_side(place, received, rows, tile):
    return pl.pallas_call(
        right_kernel,
        grid_spec=pltpu.PrefetchScalarGridSpec(
            num_scalar_prefetch=1,
            grid=(1,),
            in_specs=[pl.BlockSpec((128, 2, 8, 128), lambda i, _: (0, 0, 0, 0))]
            + [pl.BlockSpec((2, 2, 8, 1280), lambda i, _: (0, 0, 0, 0))] * 4
            + [pl.BlockSpec((8, 128), lambda i, _: (0, 0))],
            out_specs=[
                pl.BlockSpec((1024, 128), lambda i, _: (0, 0)),
                pl.BlockSpec((16, 72, 128), lambda i, _: (0, 0, 0)),
            ],
            scratch_shapes=[pltpu.VMEM((64, 128), F32)],
        ),
        out_shape=[
            jax.ShapeDtypeStruct((1024, 128), BF16),
            jax.ShapeDtypeStruct((16, 72, 128), BF16),
        ],
        name="right_side",
    )(place, received, *rows, tile)


def second_kernel(place, received, rows0, rows1, rows2, rows3, tiles, send):
    x = place[0]
    right = received[:, :64].astype(F32).reshape(16, 8, 8, 128)
    right = right.transpose(1, 0, 2, 3).reshape(1024, 128).astype(BF16)
    pieces = [
        rows[core, part, :, :1024].astype(F32)
        for part in range(2)
        for rows in (rows0, rows1, rows2, rows3)
        for core in range(2)
    ]
    left = jnp.concatenate(pieces).astype(BF16)
    product = jnp.dot(left, right, preferred_element_type=F32)
    value = fold_parts(product[:64], product[64:]).astype(BF16)
    for step in range(4):
        target = pl.multiple_of(16 * lax.rem(x - step + 4, 4), 16)
        part = value[16 * step : 16 * step + 16]
        for copy in range(64):
            send[copy, pl.ds(target, 16), :] = part
    tiles[...] = received[:, 64:].astype(F32).reshape(128, 128).astype(BF16)


def second_rows(place, received, rows):
    return pl.pallas_call(
        second_kernel,
        grid_spec=pltpu.PrefetchScalarGridSpec(
            num_scalar_prefetch=1,
            grid=(1,),
            in_specs=[pl.BlockSpec((16, 72, 128), lambda i, _: (0, 0, 0))]
            + [pl.BlockSpec((2, 2, 8, 1280), lambda i, _: (0, 0, 0, 0))] * 4,
            out_specs=[
                pl.BlockSpec((128, 128), lambda i, _: (0, 0)),
                pl.BlockSpec((64, 64, 128), lambda i, _: (0, 0, 0)),
            ],
        ),
        out_shape=[
            jax.ShapeDtypeStruct((128, 128), BF16),
            jax.ShapeDtypeStruct((64, 64, 128), BF16),
        ],
        name="second_rows",
    )(place, received, *rows)


def store_weights(weights, at, real_pairs):
    for half, (left, right) in enumerate(real_pairs):
        real, imag = pair_lanes(left, right)
        lane = 128 * half
        weights[pl.ds(at, 128), lane : lane + 128] = real.astype(BF16)
        weights[pl.ds(at, 128), 256 + lane : 384 + lane] = imag.astype(BF16)
        weights[pl.ds(at + 1024, 128), lane : lane + 128] = (-imag).astype(BF16)
        weights[pl.ds(at + 1024, 128), 256 + lane : 384 + lane] = real.astype(BF16)


def trail_product(factor, weights):
    total = jnp.dot(factor[0, 0, 0], weights[:1024], preferred_element_type=F32)
    return total + jnp.dot(factor[0, 0, 1], weights[1024:], preferred_element_type=F32)


def trail_first_kernel(place, mine, theirs, factor, rhs, out, weights):
    x = place[0]
    turn = pl.program_id(0)

    def build(blocks):
        def chunk(row, carry):
            at = pl.multiple_of(128 * row, 128)
            parts = [blocks[lax.rem(x - q + 4, 4), pl.ds(at, 128), :].astype(F32) for q in range(4)]
            store_weights(weights, at, ((parts[0], parts[1]), (parts[2], parts[3])))
            return carry

        lax.fori_loop(0, 8, chunk, 0)

    @pl.when((turn == 0) & (pl.program_id(1) == 0))
    def _():
        build(mine)

    @pl.when((turn == 1) & (pl.program_id(1) == 0))
    def _():
        build(theirs)

    total = trail_product(factor, weights)
    out[0, 0] = rhs[0, 0].astype(F32) - total[:, :256]
    out[0, 1] = rhs[0, 1].astype(F32) - total[:, 256:]


def trail_first(place, mine, theirs, trail_factor, trail_rhs):
    rows = trail_rhs.shape[2]
    height = min(256, rows)
    system = lambda turn, p: jnp.where(turn == 0, p[1], 1 - p[1])
    return pl.pallas_call(
        trail_first_kernel,
        grid_spec=pltpu.PrefetchScalarGridSpec(
            num_scalar_prefetch=1,
            grid=(2, rows // height),
            in_specs=[pl.BlockSpec((4, 1024, 128), lambda t, i, p: (0, 0, 0))] * 2
            + [
                pl.BlockSpec((1, 1, 2, height, 1024), lambda t, i, p: (system(t, p), 0, 0, i, 0)),
                pl.BlockSpec((1, 2, height, 256), lambda t, i, p: (system(t, p), 0, i, 0)),
            ],
            out_specs=pl.BlockSpec((1, 2, height, 256), lambda t, i, p: (system(t, p), 0, i, 0)),
            scratch_shapes=[pltpu.VMEM((2048, 512), BF16)],
        ),
        out_shape=jax.ShapeDtypeStruct((2, 2, rows, 256), F32),
        compiler_params=pltpu.CompilerParams(vmem_limit_bytes=VMEM_LIMIT),
        name="trail_first",
    )(place, mine, theirs, trail_factor, trail_rhs)


def trail_second_kernel(place, blocks, factor, partial, *refs):
    out, own, weights = refs[-3:]

    @pl.when(pl.program_id(0) == 0)
    def _():
        def chunk(row, carry):
            at = pl.multiple_of(128 * row, 128)
            near = pl.multiple_of(8 * row, 8)
            parts = [
                blocks[q, :, pl.ds(near, 8), :].astype(F32).reshape(128, 128) for q in range(4)
            ]
            store_weights(weights, at, ((parts[0], parts[1]), (parts[2], parts[3])))
            return carry

        lax.fori_loop(0, 8, chunk, 0)
        near = pl.multiple_of(8 * place[3], 8)
        parts = [blocks[q, place[4], pl.ds(near, 8), :].astype(F32) for q in range(4)]
        for half in range(2):
            real, imag = pair_lanes(parts[2 * half], parts[2 * half + 1])
            own[0, :, 128 * half : 128 * half + 128] = real.astype(BF16)
            own[1, :, 128 * half : 128 * half + 128] = imag.astype(BF16)

    total = trail_product(factor, weights)
    out[0, 0] = (partial[0, 0] - total[:, :256]).astype(BF16)
    out[0, 1] = (partial[0, 1] - total[:, 256:]).astype(BF16)


def trail_second(place, which, blocks, trail_factor, partial, previous=None):
    rows = partial.shape[2]
    height = min(256, rows)
    place = jnp.concatenate([place[:2], which[None], place[2:]])
    extra = () if previous is None else (previous,)
    return pl.pallas_call(
        trail_second_kernel,
        grid_spec=pltpu.PrefetchScalarGridSpec(
            num_scalar_prefetch=1,
            grid=(rows // height,),
            in_specs=[
                pl.BlockSpec((4, 16, 64, 128), lambda i, p: (0, 0, 0, 0)),
                pl.BlockSpec((1, 1, 2, height, 1024), lambda i, p: (p[2], 1, 0, i, 0)),
                pl.BlockSpec((1, 2, height, 256), lambda i, p: (p[2], 0, i, 0)),
            ]
            + [pl.BlockSpec(memory_space=pl.ANY)] * len(extra),
            out_specs=[
                pl.BlockSpec((1, 2, height, 256), lambda i, p: (p[2], 0, i, 0)),
                pl.BlockSpec((2, 8, 256), lambda i, p: (0, 0, 0)),
            ],
            scratch_shapes=[pltpu.VMEM((2048, 512), BF16)],
        ),
        out_shape=[
            jax.ShapeDtypeStruct((2, 2, rows, 256), BF16),
            jax.ShapeDtypeStruct((2, 8, 256), BF16),
        ],
        input_output_aliases={4: 0} if extra else {},
        compiler_params=pltpu.CompilerParams(vmem_limit_bytes=VMEM_LIMIT),
        name="trail_second",
    )(place, blocks, trail_factor, partial, *extra)


def spread_matrix(panel):
    spread = np.zeros((128, 3, 128), np.float32)
    for corner in range(3):
        for coordinate in range(3):
            lanes = slice(24 * corner + 8 * coordinate, 24 * corner + 8 * coordinate + 8)
            for part in range(2):
                source = 18 * part + 9 * panel + 3 * corner + coordinate
                for term in range(3):
                    spread[36 * term + source, part, lanes] = 1.0
            spread[108 + 3 * panel + corner, 2, lanes] = 32.0
            spread[114 + 3 * panel + corner, 2, lanes] = 1.0
    return jnp.asarray(spread.reshape(128, 384), BF16)


def gradient_sum(place, couple, tile_refs, spread):
    base = 8 * (16 * place[2] + place[3])
    target = (base + lax.rem(lax.broadcasted_iota(jnp.int32, (128, 128), 1), 8)).astype(F32)
    sign = jnp.where(lanes_below((128, 128), 64), 1.0, -1.0)
    total = jnp.zeros((8, 128), F32)
    for step in range(4):
        source = lax.rem(place[0] - step + 4, 4)
        for side in range(2):
            core = place[1] if side == 0 else 1 - place[1]
            same, crossed = couple(2 * source + core)
            real = jnp.sum(same * sign, axis=1, keepdims=True)
            imag = jnp.sum(crossed, axis=1, keepdims=True)
            table = jnp.dot(tile_refs[side][step], spread[...], preferred_element_type=F32)
            value = table[:, 128:256] * imag - table[:, :128] * real
            value = jnp.where(table[:, 256:] == target, value, 0.0)
            total = total + jnp.sum(value.reshape(16, 8, 128), axis=0)
    return total


def couple_pairs(pairs):
    same = jnp.zeros((128, 128), F32)
    crossed = jnp.zeros((128, 128), F32)
    for mine, theirs in pairs:
        same = same + mine * theirs
        crossed = crossed + mine * pltpu.roll(theirs, 64, 1)
    return same, crossed


def gradient_first_kernel(place, mine, theirs, own_tiles, other_tiles, spread, out):
    tiles = (own_tiles, other_tiles)

    def couple(row):
        at = pl.multiple_of(128 * row, 128)
        return couple_pairs(
            (mine[q, pl.ds(at, 128), :].astype(F32), theirs[q, pl.ds(at, 128), :].astype(F32))
            for q in range(4)
        )

    out[...] = gradient_sum(place, couple, tiles, spread)


def gradient_first(place, mine, theirs, tiles, spread):
    return pl.pallas_call(
        gradient_first_kernel,
        grid_spec=pltpu.PrefetchScalarGridSpec(
            num_scalar_prefetch=1,
            grid=(1,),
            in_specs=[pl.BlockSpec((4, 1024, 128), lambda i, p: (0, 0, 0))] * 2
            + [pl.BlockSpec((4, 128, 128), lambda i, p: (0, 0, 0))] * 2
            + [pl.BlockSpec((128, 384), lambda i, p: (0, 0))],
            out_specs=pl.BlockSpec((8, 128), lambda i, p: (0, 0)),
        ),
        out_shape=jax.ShapeDtypeStruct((8, 128), F32),
        compiler_params=pltpu.CompilerParams(vmem_limit_bytes=VMEM_LIMIT),
        name="gradient_first",
    )(place, mine, theirs, *tiles, spread)


def gradient_second_kernel(place, mine, theirs, own_tiles, other_tiles, spread, before, out):
    tiles = (own_tiles, other_tiles)

    def couple(row):
        near = pl.multiple_of(8 * row, 8)
        return couple_pairs(
            (
                mine[q, :, pl.ds(near, 8), :].astype(F32).reshape(128, 128),
                theirs[q, :, pl.ds(near, 8), :].astype(F32).reshape(128, 128),
            )
            for q in range(4)
        )

    total = before[...] + gradient_sum(place, couple, tiles, spread)
    total = jnp.sum(total, axis=0, keepdims=True)
    total = total + pltpu.roll(total, 104, 1) + pltpu.roll(total, 80, 1)
    for coordinate in range(3):
        out[coordinate : coordinate + 1, :] = total[:, 8 * coordinate : 8 * coordinate + 8]


def gradient_second(place, mine, theirs, tiles, spread, before):
    return pl.pallas_call(
        gradient_second_kernel,
        grid_spec=pltpu.PrefetchScalarGridSpec(
            num_scalar_prefetch=1,
            grid=(1,),
            in_specs=[pl.BlockSpec((4, 16, 64, 128), lambda i, p: (0, 0, 0, 0))] * 2
            + [pl.BlockSpec((4, 128, 128), lambda i, p: (0, 0, 0))] * 2
            + [
                pl.BlockSpec((128, 384), lambda i, p: (0, 0)),
                pl.BlockSpec((8, 128), lambda i, p: (0, 0)),
            ],
            out_specs=pl.BlockSpec((3, 8), lambda i, p: (0, 0)),
        ),
        out_shape=jax.ShapeDtypeStruct((3, 8), F32),
        compiler_params=pltpu.CompilerParams(vmem_limit_bytes=VMEM_LIMIT),
        name="gradient_second",
    )(place, mine, theirs, *tiles, spread, before)


def rounds_x(value):
    sent = [lax.ppermute(value, "x", [(i, (i + step) % 4) for i in range(4)]) for step in (1, 2, 3)]
    return [value, *sent]


def swap_core(value):
    return lax.ppermute(value, "core", [(0, 1), (1, 0)])


def element_tile(shape_tiles, element_vertices, vertex_slot):
    values = shape_tiles.transpose(3, 0, 2, 1).reshape(8, 36)
    high = lax.reduce_precision(values, 8, 7)
    rest = values - high
    mid = lax.reduce_precision(rest, 8, 7)
    low = rest - mid
    slots = vertex_slot[element_vertices].transpose(1, 0, 2).reshape(8, 6)
    parts = [high, mid, low, (slots // 32).astype(F32), (slots % 32).astype(F32), jnp.zeros((8, 8), F32)]
    return jnp.concatenate(parts, axis=1).astype(BF16)


def steps(
    panel_inverse,
    panel_below,
    trail_factor,
    first_rhs,
    second_rhs,
    trail_rhs,
    shape_tiles,
    element_vertices,
    vertex_slot,
):
    x = lax.axis_index("x")
    core = lax.axis_index("core")
    col = lax.axis_index("col")
    place = jnp.stack([x, core, 2 * x + core, col]).astype(jnp.int32)

    first, send, own, give = prepare(place, panel_inverse, first_rhs, panel_below, second_rhs)
    received = lax.all_to_all(send.reshape(128, 2, 8, 128), ALL, 0, 0, tiled=True)

    other = swap_core(give)
    chip = jnp.where(core == 0, jnp.stack([own, other]), jnp.stack([other, own]))
    rows = rounds_x(chip)
    tile = element_tile(shape_tiles, element_vertices, vertex_slot)

    first_block, send = right_side(place, received, rows, tile)
    received = lax.all_to_all(send, "col", 0, 0, tiled=True)
    first_mine = rounds_x(first_block)
    first_mine = jnp.stack(first_mine)
    first_theirs = swap_core(first_mine)

    tiles, send = second_rows(place, received, rows)
    second_mine = lax.all_to_all(send, ("x", "col"), 0, 0, tiled=True)

    tiles = rounds_x(tiles)
    tiles = jnp.stack(tiles)
    tiles = (tiles, swap_core(tiles))
    partial = trail_first(place, first_mine, first_theirs, trail_factor, trail_rhs)
    gradient = gradient_first(place, first_mine, first_theirs, tiles, spread_matrix(0))

    second_theirs = swap_core(second_mine)
    mine = second_mine.reshape(4, 16, 64, 128)
    theirs = second_theirs.reshape(4, 16, 64, 128)
    update, own_mine = trail_second(place, core, mine, trail_factor, partial)
    update, own_theirs = trail_second(place, 1 - core, theirs, trail_factor, partial, update)
    gradient = gradient_second(place, mine, theirs, tiles, spread_matrix(1), gradient)

    second = jnp.where(
        core == 0, jnp.stack([own_mine, own_theirs]), jnp.stack([own_theirs, own_mine])
    )
    return (jnp.stack([first, second], axis=1), update, gradient)


def solution(mesh):
    fine = Mesh(mesh.devices.reshape(4, 2, 16), ALL)
    return jax.shard_map(
        steps,
        mesh=fine,
        in_specs=(
            P(None, None, None, ALL, None),
            P(None, None, ALL, None),
            P(None, None, None, ALL, None),
            P(),
            P(None, None, ALL, None),
            P(None, None, ALL, None),
            P(None, None, None, ALL),
            P(None, ALL, None),
            P(),
        ),
        out_specs=(
            P(None, None, None, ALL, None),
            P(None, None, ALL, None),
            P(None, ALL),
        ),
        check_vma=False,
    )
```

```python
import jax
import jax.numpy as jnp
import numpy as np
from jax import lax
from jax.experimental import pallas as pl
from jax.experimental.pallas import tpu as pltpu
from jax.sharding import Mesh
from jax.sharding import PartitionSpec as P


ALL = ("x", "core", "col")
F32 = jnp.float32
BF16 = jnp.bfloat16
VMEM_LIMIT = 48 * 1024 * 1024
HEIGHT = 256


def lanes_below(shape, bound):
    return lax.broadcasted_iota(jnp.int32, shape, len(shape) - 1) < bound


def pair_lanes(left, right):
    low = lanes_below(left.shape, 64)
    real = jnp.where(low, left, pltpu.roll(right, 64, 1))
    imag = jnp.where(low, pltpu.roll(left, 64, 1), right)
    return real, imag


def fold_parts(top, low):
    turned = pltpu.roll(low, 64, 1)
    return top + jnp.where(lanes_below(low.shape, 64), -turned, turned)


def prepare_kernel(place, inverse, rhs, below, own_rhs, first, send, own, give):
    system = pl.program_id(0)
    left = jnp.concatenate([inverse[0, 0, 0].astype(F32), inverse[0, 0, 1].astype(F32)]).astype(BF16)
    by_real = jnp.dot(left, rhs[0, 0], preferred_element_type=F32)
    by_imag = jnp.dot(left, rhs[0, 1], preferred_element_type=F32)
    real = (by_real[:8] - by_imag[8:]).astype(BF16)
    imag = (by_imag[:8] + by_real[8:]).astype(BF16)
    first[0, 0] = real
    first[0, 1] = imag
    real = real.astype(F32)
    imag = imag.astype(F32)
    for half in range(2):
        cut = slice(128 * half, 128 * half + 128)
        even, odd = pair_lanes(real[:, cut], imag[:, cut])
        for group, value in ((2 * half, even), (2 * half + 1, odd)):
            value = value.astype(BF16)
            for col in range(16):
                send[group, 0, col, 0] = value
    lane_block = lax.broadcasted_iota(jnp.int32, (8, 128), 1) // 8
    pieces = [
        below[0, part, :, 128 * row : 128 * row + 128].astype(F32)
        for part in range(2)
        for row in range(8)
    ]
    for col in range(16):
        value = pltpu.roll(pieces[0], (128 - 8 * col) % 128, 1)
        for block in range(1, 16):
            turned = pltpu.roll(pieces[block], (8 * block - 8 * col) % 128, 1)
            value = jnp.where(lane_block == block, turned, value)
        value = value.astype(BF16)
        for group in range(4):
            send[group, 0, col, 1] = value

    def fill(target):
        for part in range(2):
            target[part, :, :1024] = inverse[0, 1, part]
            target[part, :, 1024:] = own_rhs[0, part]

    @pl.when(system == place[1])
    def _():
        fill(own)

    @pl.when(system != place[1])
    def _():
        fill(give)


def prepare(place, panel_inverse, first_rhs, panel_below, second_rhs):
    return pl.pallas_call(
        prepare_kernel,
        grid_spec=pltpu.PrefetchScalarGridSpec(
            num_scalar_prefetch=1,
            grid=(2,),
            in_specs=[
                pl.BlockSpec((1, 2, 2, 8, 1024), lambda s, _: (s, 0, 0, 0, 0)),
                pl.BlockSpec((1, 2, 1024, 256), lambda s, _: (s, 0, 0, 0)),
                pl.BlockSpec((1, 2, 8, 1024), lambda s, _: (s, 0, 0, 0)),
                pl.BlockSpec((1, 2, 8, 256), lambda s, _: (s, 0, 0, 0)),
            ],
            out_specs=[
                pl.BlockSpec((1, 2, 8, 256), lambda s, _: (s, 0, 0, 0)),
                pl.BlockSpec((4, 1, 16, 2, 8, 128), lambda s, _: (0, s, 0, 0, 0, 0)),
                pl.BlockSpec((2, 8, 1280), lambda s, _: (0, 0, 0)),
                pl.BlockSpec((2, 8, 1280), lambda s, _: (0, 0, 0)),
            ],
        ),
        out_shape=[
            jax.ShapeDtypeStruct((2, 2, 8, 256), BF16),
            jax.ShapeDtypeStruct((4, 2, 16, 2, 8, 128), BF16),
            jax.ShapeDtypeStruct((2, 8, 1280), BF16),
            jax.ShapeDtypeStruct((2, 8, 1280), BF16),
        ],
        name="prepare",
    )(place, panel_inverse, first_rhs, panel_below, second_rhs)


def right_kernel(place, received, rows0, rows1, rows2, rows3, block, send, offset):
    x = place[0]
    half = pl.multiple_of(1024 + 128 * (x // 2), 128)
    odd = x % 2 == 1
    for step, rows in enumerate((rows0, rows1, rows2, rows3)):
        source = lax.rem(x - step + 4, 4)
        for core in range(2):
            real = rows[core, 0, :, pl.ds(half, 128)].astype(F32)
            imag = rows[core, 1, :, pl.ds(half, 128)].astype(F32)
            even_pair, odd_pair = pair_lanes(real, imag)
            value = jnp.where(odd, odd_pair, even_pair)
            offset[pl.ds(pl.multiple_of(16 * source + 8 * core, 8), 8), :] = value
    first = received[:, 0].astype(F32).reshape(1024, 128).astype(BF16)
    below = received[:, 1].astype(F32).reshape(1024, 128).astype(BF16)
    block[...] = first
    product = lax.dot_general(below, first, (((0,), (0,)), ((), ())), preferred_element_type=F32)
    right = (offset[...] - fold_parts(product[:64], product[64:])).astype(BF16)
    for col in range(16):
        send[col] = right


def right_side(place, received, rows):
    return pl.pallas_call(
        right_kernel,
        grid_spec=pltpu.PrefetchScalarGridSpec(
            num_scalar_prefetch=1,
            grid=(1,),
            in_specs=[pl.BlockSpec((128, 2, 8, 128), lambda i, _: (0, 0, 0, 0))]
            + [pl.BlockSpec((2, 2, 8, 1280), lambda i, _: (0, 0, 0, 0))] * 4,
            out_specs=[
                pl.BlockSpec((1024, 128), lambda i, _: (0, 0)),
                pl.BlockSpec((16, 64, 128), lambda i, _: (0, 0, 0)),
            ],
            scratch_shapes=[pltpu.VMEM((64, 128), F32)],
        ),
        out_shape=[
            jax.ShapeDtypeStruct((1024, 128), BF16),
            jax.ShapeDtypeStruct((16, 64, 128), BF16),
        ],
        name="right_side",
    )(place, received, *rows)


def second_kernel(place, received, rows0, rows1, rows2, rows3, tile, send):
    x = place[0]
    right = received[...].astype(F32).reshape(16, 8, 8, 128)
    right = right.transpose(1, 0, 2, 3).reshape(1024, 128).astype(BF16)
    pieces = [
        rows[core, part, :, :1024].astype(F32)
        for part in range(2)
        for rows in (rows0, rows1, rows2, rows3)
        for core in range(2)
    ]
    left = jnp.concatenate(pieces).astype(BF16)
    product = jnp.dot(left, right, preferred_element_type=F32)
    value = fold_parts(product[:64], product[64:]).astype(BF16)
    for step in range(4):
        target = pl.multiple_of(16 * lax.rem(x - step + 4, 4), 16)
        part = value[16 * step : 16 * step + 16]
        for copy in range(64):
            send[copy, pl.ds(target, 16), :] = part
    for copy in range(64):
        send[copy, 64:] = tile[...]


def second_rows(place, received, rows, tile):
    return pl.pallas_call(
        second_kernel,
        grid_spec=pltpu.PrefetchScalarGridSpec(
            num_scalar_prefetch=1,
            grid=(1,),
            in_specs=[pl.BlockSpec((16, 64, 128), lambda i, _: (0, 0, 0))]
            + [pl.BlockSpec((2, 2, 8, 1280), lambda i, _: (0, 0, 0, 0))] * 4
            + [pl.BlockSpec((8, 128), lambda i, _: (0, 0))],
            out_specs=pl.BlockSpec((64, 72, 128), lambda i, _: (0, 0, 0)),
        ),
        out_shape=jax.ShapeDtypeStruct((64, 72, 128), BF16),
        name="second_rows",
    )(place, received, *rows, tile)


def trail_product(factor, blocks):
    height = factor.shape[3]
    stacked = factor[0, 0].reshape(2 * height, 1024)
    product = jnp.dot(stacked, blocks[...], preferred_element_type=F32)
    real, imag = [], []
    for half in range(2):
        lanes = slice(256 * half, 256 * half + 128)
        even, even_turned = product[:height, lanes], product[height:, lanes]
        lanes = slice(256 * half + 128, 256 * half + 256)
        odd, odd_turned = product[:height, lanes], product[height:, lanes]
        low = lanes_below(even.shape, 64)
        turn = lambda value: pltpu.roll(value, 64, 1)
        real.append(jnp.where(low, even - turn(even_turned), turn(odd) - odd_turned))
        imag.append(jnp.where(low, turn(even) + even_turned, odd + turn(odd_turned)))
    return jnp.concatenate(real, axis=1), jnp.concatenate(imag, axis=1)


def trail_first_kernel(place, mine, theirs, factor, rhs, out, blocks):
    x = place[0]
    turn = pl.program_id(0)

    @pl.when((turn == 0) & (pl.program_id(1) == 0))
    def _():
        for q in range(4):
            blocks[:, 128 * q : 128 * q + 128] = mine[lax.rem(x - q + 4, 4)]

    @pl.when((turn == 1) & (pl.program_id(1) == 0))
    def _():
        for q in range(4):
            blocks[:, 128 * q : 128 * q + 128] = theirs[lax.rem(x - q + 4, 4)]

    real, imag = trail_product(factor, blocks)
    out[0, 0] = rhs[0, 0].astype(F32) - real
    out[0, 1] = rhs[0, 1].astype(F32) - imag


def trail_first(place, mine, theirs, trail_factor, trail_rhs):
    rows = trail_rhs.shape[2]
    height = min(HEIGHT, rows)
    system = lambda turn, p: jnp.where(turn == 0, p[1], 1 - p[1])
    return pl.pallas_call(
        trail_first_kernel,
        grid_spec=pltpu.PrefetchScalarGridSpec(
            num_scalar_prefetch=1,
            grid=(2, rows // height),
            in_specs=[pl.BlockSpec((4, 1024, 128), lambda t, i, p: (0, 0, 0))] * 2
            + [
                pl.BlockSpec((1, 1, 2, height, 1024), lambda t, i, p: (system(t, p), 0, 0, i, 0)),
                pl.BlockSpec((1, 2, height, 256), lambda t, i, p: (system(t, p), 0, i, 0)),
            ],
            out_specs=pl.BlockSpec((1, 2, height, 256), lambda t, i, p: (system(t, p), 0, i, 0)),
            scratch_shapes=[pltpu.VMEM((1024, 512), BF16)],
        ),
        out_shape=jax.ShapeDtypeStruct((2, 2, rows, 256), F32),
        compiler_params=pltpu.CompilerParams(vmem_limit_bytes=VMEM_LIMIT),
        name="trail_first",
    )(place, mine, theirs, trail_factor, trail_rhs)


def trail_second_kernel(place, received, factor, partial, *refs):
    out, own, blocks = refs[-3:]

    @pl.when(pl.program_id(0) == 0)
    def _():
        for q in range(4):
            for row in range(8):
                value = received[q, :, 8 * row : 8 * row + 8, :].astype(F32).reshape(128, 128)
                blocks[128 * row : 128 * row + 128, 128 * q : 128 * q + 128] = value.astype(BF16)
        near = pl.multiple_of(8 * place[3], 8)
        parts = [received[q, place[4], pl.ds(near, 8), :].astype(F32) for q in range(4)]
        for half in range(2):
            real, imag = pair_lanes(parts[2 * half], parts[2 * half + 1])
            own[0, :, 128 * half : 128 * half + 128] = real.astype(BF16)
            own[1, :, 128 * half : 128 * half + 128] = imag.astype(BF16)

    real, imag = trail_product(factor, blocks)
    out[0, 0] = (partial[0, 0] - real).astype(BF16)
    out[0, 1] = (partial[0, 1] - imag).astype(BF16)


def trail_second(place, which, received, trail_factor, partial, previous=None):
    rows = partial.shape[2]
    height = min(HEIGHT, rows)
    place = jnp.concatenate([place[:2], which[None], place[2:]])
    extra = () if previous is None else (previous,)
    return pl.pallas_call(
        trail_second_kernel,
        grid_spec=pltpu.PrefetchScalarGridSpec(
            num_scalar_prefetch=1,
            grid=(rows // height,),
            in_specs=[
                pl.BlockSpec((4, 16, 72, 128), lambda i, p: (0, 0, 0, 0)),
                pl.BlockSpec((1, 1, 2, height, 1024), lambda i, p: (p[2], 1, 0, i, 0)),
                pl.BlockSpec((1, 2, height, 256), lambda i, p: (p[2], 0, i, 0)),
            ]
            + [pl.BlockSpec(memory_space=pl.ANY)] * len(extra),
            out_specs=[
                pl.BlockSpec((1, 2, height, 256), lambda i, p: (p[2], 0, i, 0)),
                pl.BlockSpec((2, 8, 256), lambda i, p: (0, 0, 0)),
            ],
            scratch_shapes=[pltpu.VMEM((1024, 512), BF16)],
        ),
        out_shape=[
            jax.ShapeDtypeStruct((2, 2, rows, 256), BF16),
            jax.ShapeDtypeStruct((2, 8, 256), BF16),
        ],
        input_output_aliases={4: 0} if extra else {},
        compiler_params=pltpu.CompilerParams(vmem_limit_bytes=VMEM_LIMIT),
        name="trail_second",
    )(place, received, trail_factor, partial, *extra)


def spread_matrix():
    spread = np.zeros((128, 2, 3, 128), np.float32)
    for panel in range(2):
        for corner in range(3):
            for coordinate in range(3):
                lanes = slice(24 * corner + 8 * coordinate, 24 * corner + 8 * coordinate + 8)
                for part in range(2):
                    source = 18 * part + 9 * panel + 3 * corner + coordinate
                    for term in range(3):
                        spread[36 * term + source, panel, part, lanes] = 1.0
                spread[108 + 3 * panel + corner, panel, 2, lanes] = 32.0
                spread[114 + 3 * panel + corner, panel, 2, lanes] = 1.0
    return jnp.asarray(spread.reshape(128, 768), BF16)


def couple(pairs):
    same = jnp.zeros((128, 128), F32)
    crossed = jnp.zeros((128, 128), F32)
    for mine, theirs in pairs:
        mine = mine.astype(F32).reshape(128, 128)
        theirs = theirs.astype(F32).reshape(128, 128)
        same = same + mine * theirs
        crossed = crossed + mine * pltpu.roll(theirs, 64, 1)
    low = lanes_below((128, 128), 64)
    real = jnp.sum(jnp.where(low, same, -same), axis=1, keepdims=True)
    imag = jnp.sum(crossed, axis=1, keepdims=True)
    return real, imag


def couple_first_kernel(mine, theirs, out):
    low = lanes_below((128, 128), 64)
    for row in range(8):
        cut = slice(128 * row, 128 * row + 128)
        real, imag = couple((mine[q, cut, :], theirs[q, cut, :]) for q in range(4))
        out[cut, :] = jnp.where(low, real, imag)


def couple_first(mine, theirs):
    return pl.pallas_call(
        couple_first_kernel,
        out_shape=jax.ShapeDtypeStruct((1024, 128), F32),
        compiler_params=pltpu.CompilerParams(vmem_limit_bytes=VMEM_LIMIT),
        name="couple_first",
    )(mine, theirs)


def gradient_kernel(place, mine, theirs, before, spread, out):
    base = 8 * (16 * place[2] + place[3])
    target = (base + lax.rem(lax.broadcasted_iota(jnp.int32, (128, 128), 1), 8)).astype(F32)
    total = jnp.zeros((8, 128), F32)
    for source in range(4):
        for side in range(2):
            near, _ = (mine, theirs) if side == 0 else (theirs, mine)
            row = 2 * source + (place[1] if side == 0 else 1 - place[1])
            cut = pl.ds(pl.multiple_of(8 * row, 8), 8)
            real, imag = couple((mine[q, :, cut, :], theirs[q, :, cut, :]) for q in range(4))
            first = before[pl.ds(pl.multiple_of(128 * row, 128), 128), :]
            tile = near[source, :, 64:, :].astype(F32).reshape(128, 128).astype(BF16)
            table = jnp.dot(tile, spread[...], preferred_element_type=F32)
            for at, real, imag in ((0, first[:, :1], first[:, 64:65]), (384, real, imag)):
                value = table[:, at + 128 : at + 256] * imag - table[:, at : at + 128] * real
                value = jnp.where(table[:, at + 256 : at + 384] == target, value, 0.0)
                total = total + jnp.sum(value.reshape(16, 8, 128), axis=0)
    total = jnp.sum(total, axis=0, keepdims=True)
    total = total + pltpu.roll(total, 104, 1) + pltpu.roll(total, 80, 1)
    for coordinate in range(3):
        out[coordinate : coordinate + 1, :] = total[:, 8 * coordinate : 8 * coordinate + 8]


def gradient_of(place, mine, theirs, before, spread):
    return pl.pallas_call(
        gradient_kernel,
        grid_spec=pltpu.PrefetchScalarGridSpec(
            num_scalar_prefetch=1,
            grid=(1,),
            in_specs=[pl.BlockSpec((4, 16, 72, 128), lambda i, p: (0, 0, 0, 0))] * 2
            + [
                pl.BlockSpec((1024, 128), lambda i, p: (0, 0)),
                pl.BlockSpec((128, 768), lambda i, p: (0, 0)),
            ],
            out_specs=pl.BlockSpec((3, 8), lambda i, p: (0, 0)),
        ),
        out_shape=jax.ShapeDtypeStruct((3, 8), F32),
        compiler_params=pltpu.CompilerParams(vmem_limit_bytes=VMEM_LIMIT),
        name="gradient",
    )(place, mine, theirs, before, spread)


def rounds_x(value):
    sent = [lax.ppermute(value, "x", [(i, (i + step) % 4) for i in range(4)]) for step in (1, 2, 3)]
    return [value, *sent]


def swap_core(value):
    return lax.ppermute(value, "core", [(0, 1), (1, 0)])


def element_tile(shape_tiles, element_vertices, vertex_slot):
    values = shape_tiles.transpose(3, 0, 2, 1).reshape(8, 36)
    high = lax.reduce_precision(values, 8, 7)
    rest = values - high
    mid = lax.reduce_precision(rest, 8, 7)
    low = rest - mid
    slots = vertex_slot[element_vertices].transpose(1, 0, 2).reshape(8, 6)
    parts = [high, mid, low, (slots // 32).astype(F32), (slots % 32).astype(F32), jnp.zeros((8, 8), F32)]
    return jnp.concatenate(parts, axis=1).astype(BF16)


def steps(
    panel_inverse,
    panel_below,
    trail_factor,
    first_rhs,
    second_rhs,
    trail_rhs,
    shape_tiles,
    element_vertices,
    vertex_slot,
):
    x = lax.axis_index("x")
    core = lax.axis_index("core")
    col = lax.axis_index("col")
    place = jnp.stack([x, core, 2 * x + core, col]).astype(jnp.int32)

    first, send, own, give = prepare(place, panel_inverse, first_rhs, panel_below, second_rhs)
    received = lax.all_to_all(send.reshape(128, 2, 8, 128), ALL, 0, 0, tiled=True)

    other = swap_core(give)
    chip = jnp.where(core == 0, jnp.stack([own, other]), jnp.stack([other, own]))
    rows = rounds_x(chip)
    tile = element_tile(shape_tiles, element_vertices, vertex_slot)

    first_block, send = right_side(place, received, rows)
    received = lax.all_to_all(send, "col", 0, 0, tiled=True)
    first_mine = rounds_x(first_block)
    first_mine = jnp.stack(first_mine)
    first_theirs = swap_core(first_mine)

    send = second_rows(place, received, rows, tile)
    second_mine = lax.all_to_all(send, ("x", "col"), 0, 0, tiled=True)

    partial = trail_first(place, first_mine, first_theirs, trail_factor, trail_rhs)
    partial = pltpu.with_memory_space_constraint(partial, pltpu.HBM)
    before = couple_first(first_mine, first_theirs)

    second_theirs = swap_core(second_mine)
    mine = second_mine.reshape(4, 16, 72, 128)
    theirs = second_theirs.reshape(4, 16, 72, 128)
    update, own_mine = trail_second(place, core, mine, trail_factor, partial)
    update, own_theirs = trail_second(place, 1 - core, theirs, trail_factor, partial, update)
    gradient = gradient_of(place, mine, theirs, before, spread_matrix())

    second = jnp.where(
        core == 0, jnp.stack([own_mine, own_theirs]), jnp.stack([own_theirs, own_mine])
    )
    return (jnp.stack([first, second], axis=1), update, gradient)


def solution(mesh):
    fine = Mesh(mesh.devices.reshape(4, 2, 16), ALL)
    return jax.shard_map(
        steps,
        mesh=fine,
        in_specs=(
            P(None, None, None, ALL, None),
            P(None, None, ALL, None),
            P(None, None, None, ALL, None),
            P(),
            P(None, None, ALL, None),
            P(None, None, ALL, None),
            P(None, None, None, ALL),
            P(None, ALL, None),
            P(),
        ),
        out_specs=(
            P(None, None, None, ALL, None),
            P(None, None, ALL, None),
            P(None, ALL),
        ),
        check_vma=False,
    )
```

```python
import jax
import jax.numpy as jnp
import numpy as np
from jax import lax
from jax.experimental import pallas as pl
from jax.experimental.pallas import tpu as pltpu
from jax.sharding import Mesh
from jax.sharding import PartitionSpec as P


ALL = ("x", "core", "col")
F32 = jnp.float32
BF16 = jnp.bfloat16
TRAIL_VMEM = 24 * 1024 * 1024
SMALL_VMEM = 12 * 1024 * 1024
SPACE = pltpu.VMEM


def lanes_below(shape, bound):
    return lax.broadcasted_iota(jnp.int32, shape, len(shape) - 1) < bound


def pair_lanes(left, right):
    low = lanes_below(left.shape, 64)
    real = jnp.where(low, left, pltpu.roll(right, 64, 1))
    imag = jnp.where(low, pltpu.roll(left, 64, 1), right)
    return real, imag


def fold_parts(top, low):
    turned = pltpu.roll(low, 64, 1)
    return top + jnp.where(lanes_below(low.shape, 64), -turned, turned)


def prepare_kernel(inverse, rhs, below, own_rhs, first, send, own, give):
    system = pl.program_id(0)
    core = lax.axis_index("core")
    left = jnp.concatenate([inverse[0, 0, 0].astype(F32), inverse[0, 0, 1].astype(F32)]).astype(BF16)
    by_real = jnp.dot(left, rhs[0, 0], preferred_element_type=F32)
    by_imag = jnp.dot(left, rhs[0, 1], preferred_element_type=F32)
    real = (by_real[:8] - by_imag[8:]).astype(BF16)
    imag = (by_imag[:8] + by_real[8:]).astype(BF16)
    first[0, 0] = real
    first[0, 1] = imag
    real = real.astype(F32)
    imag = imag.astype(F32)
    for half in range(2):
        cut = slice(128 * half, 128 * half + 128)
        even, odd = pair_lanes(real[:, cut], imag[:, cut])
        for group, value in ((2 * half, even), (2 * half + 1, odd)):
            value = value.astype(BF16)
            for col in range(16):
                send[group, 0, col, 0] = value
    lane_block = lax.broadcasted_iota(jnp.int32, (8, 128), 1) // 8
    pieces = [
        below[0, part, :, 128 * row : 128 * row + 128].astype(F32)
        for part in range(2)
        for row in range(8)
    ]
    for col in range(16):
        value = pltpu.roll(pieces[0], (128 - 8 * col) % 128, 1)
        for block in range(1, 16):
            turned = pltpu.roll(pieces[block], (8 * block - 8 * col) % 128, 1)
            value = jnp.where(lane_block == block, turned, value)
        value = value.astype(BF16)
        for group in range(4):
            send[group, 0, col, 1] = value

    def fill(target):
        for part in range(2):
            target[part, :, :1024] = inverse[0, 1, part]
            target[part, :, 1024:] = own_rhs[0, part]

    @pl.when(system == core)
    def _():
        fill(own)

    @pl.when(system != core)
    def _():
        fill(give)


def prepare(panel_inverse, first_rhs, panel_below, second_rhs):
    return pl.pallas_call(
        prepare_kernel,
        grid=(2,),
        in_specs=[
            pl.BlockSpec((1, 2, 2, 8, 1024), lambda s: (s, 0, 0, 0, 0)),
            pl.BlockSpec((1, 2, 1024, 256), lambda s: (s, 0, 0, 0)),
            pl.BlockSpec((1, 2, 8, 1024), lambda s: (s, 0, 0, 0)),
            pl.BlockSpec((1, 2, 8, 256), lambda s: (s, 0, 0, 0)),
        ],
        out_specs=[
            pl.BlockSpec((1, 2, 8, 256), lambda s: (s, 0, 0, 0)),
            pl.BlockSpec((4, 1, 16, 2, 8, 128), lambda s: (0, s, 0, 0, 0, 0)),
            pl.BlockSpec((2, 8, 1280), lambda s: (0, 0, 0)),
            pl.BlockSpec((2, 8, 1280), lambda s: (0, 0, 0)),
        ],
        out_shape=[
            jax.ShapeDtypeStruct((2, 2, 8, 256), BF16),
            jax.ShapeDtypeStruct((4, 2, 16, 2, 8, 128), BF16),
            jax.ShapeDtypeStruct((2, 8, 1280), BF16),
            jax.ShapeDtypeStruct((2, 8, 1280), BF16),
        ],
        compiler_params=pltpu.CompilerParams(vmem_limit_bytes=SMALL_VMEM),
        name="prepare",
    )(panel_inverse, first_rhs, panel_below, second_rhs)


def right_kernel(place, received, rows0, rows1, rows2, rows3, block, send, offset):
    x = place[0]
    half = pl.multiple_of(1024 + 128 * (x // 2), 128)
    odd = x % 2 == 1
    for step, rows in enumerate((rows0, rows1, rows2, rows3)):
        source = lax.rem(x - step + 4, 4)
        for core in range(2):
            real = rows[core, 0, :, pl.ds(half, 128)].astype(F32)
            imag = rows[core, 1, :, pl.ds(half, 128)].astype(F32)
            even_pair, odd_pair = pair_lanes(real, imag)
            value = jnp.where(odd, odd_pair, even_pair)
            offset[pl.ds(pl.multiple_of(16 * source + 8 * core, 8), 8), :] = value
    first = received[:, 0].astype(F32).reshape(1024, 128).astype(BF16)
    below = received[:, 1].astype(F32).reshape(1024, 128).astype(BF16)
    block[...] = first
    product = lax.dot_general(below, first, (((0,), (0,)), ((), ())), preferred_element_type=F32)
    right = (offset[...] - fold_parts(product[:64], product[64:])).astype(BF16)
    for col in range(16):
        send[col] = right


def right_side(place, received, rows):
    inside = pl.BlockSpec(memory_space=pltpu.VMEM)
    return pl.pallas_call(
        right_kernel,
        in_specs=[pl.BlockSpec(memory_space=pltpu.SMEM)] + [inside] * 5,
        out_specs=[inside] * 2,
        out_shape=[SPACE((1024, 128), BF16), SPACE((16, 64, 128), BF16)],
        scratch_shapes=[pltpu.VMEM((64, 128), F32)],
        compiler_params=pltpu.CompilerParams(vmem_limit_bytes=SMALL_VMEM),
        name="right_side",
    )(place, received, *rows)


def second_kernel(place, received, rows0, rows1, rows2, rows3, tile, send):
    x = place[0]
    right = received[...].astype(F32).reshape(16, 8, 8, 128)
    right = right.transpose(1, 0, 2, 3).reshape(1024, 128).astype(BF16)
    pieces = [
        rows[core, part, :, :1024].astype(F32)
        for part in range(2)
        for rows in (rows0, rows1, rows2, rows3)
        for core in range(2)
    ]
    left = jnp.concatenate(pieces).astype(BF16)
    product = jnp.dot(left, right, preferred_element_type=F32)
    value = fold_parts(product[:64], product[64:]).astype(BF16)
    for step in range(4):
        target = pl.multiple_of(16 * lax.rem(x - step + 4, 4), 16)
        part = value[16 * step : 16 * step + 16]
        for copy in range(64):
            send[copy, pl.ds(target, 16), :] = part
    for copy in range(64):
        send[copy, 64:] = tile[...]


def second_rows(place, received, rows, tile):
    inside = pl.BlockSpec(memory_space=pltpu.VMEM)
    return pl.pallas_call(
        second_kernel,
        in_specs=[pl.BlockSpec(memory_space=pltpu.SMEM)] + [inside] * 6,
        out_specs=inside,
        out_shape=SPACE((64, 72, 128), BF16),
        compiler_params=pltpu.CompilerParams(vmem_limit_bytes=SMALL_VMEM),
        name="second_rows",
    )(place, received, *rows, tile)


def trail_product(stacked, blocks):
    height = stacked.shape[0] // 2
    product = jnp.dot(stacked, blocks[...], preferred_element_type=F32)
    real, imag = [], []
    for half in range(2):
        lanes = slice(256 * half, 256 * half + 128)
        even, even_turned = product[:height, lanes], product[height:, lanes]
        lanes = slice(256 * half + 128, 256 * half + 256)
        odd, odd_turned = product[:height, lanes], product[height:, lanes]
        low = lanes_below(even.shape, 64)
        turn = lambda value: pltpu.roll(value, 64, 1)
        real.append(jnp.where(low, even - turn(even_turned), turn(odd) - odd_turned))
        imag.append(jnp.where(low, turn(even) + even_turned, odd + turn(odd_turned)))
    return jnp.concatenate(real, axis=1), jnp.concatenate(imag, axis=1)


def trail_first_kernel(place, mine, theirs, factor, rhs, near, far, blocks):
    x = place[0]
    turn = pl.program_id(0)
    step = pl.program_id(1)
    system = jnp.where(turn == 0, place[1], 1 - place[1])

    @pl.when((turn == 0) & (step == 0))
    def _():
        for q in range(4):
            blocks[:, 128 * q : 128 * q + 128] = mine[lax.rem(x - q + 4, 4)]

    @pl.when((turn == 1) & (step == 0))
    def _():
        for q in range(4):
            blocks[:, 128 * q : 128 * q + 128] = theirs[lax.rem(x - q + 4, 4)]

    height = factor.shape[3]
    real, imag = trail_product(factor[0, 0].reshape(2 * height, 1024), blocks)
    real = rhs[0, 0].astype(F32) - real
    imag = rhs[0, 1].astype(F32) - imag

    @pl.when(step < 3)
    def _():
        rows = pl.ds(pl.multiple_of(height * step, height), height)
        near[system, 0, rows, :] = real
        near[system, 1, rows, :] = imag

    @pl.when(step == 3)
    def _():
        far[0, 0] = real
        far[0, 1] = imag


def trail_first(place, mine, theirs, trail_factor, trail_rhs):
    rows = trail_rhs.shape[2]
    height = rows // 4
    system = lambda turn, p: jnp.where(turn == 0, p[1], 1 - p[1])
    return pl.pallas_call(
        trail_first_kernel,
        grid_spec=pltpu.PrefetchScalarGridSpec(
            num_scalar_prefetch=1,
            grid=(2, 4),
            in_specs=[pl.BlockSpec((4, 1024, 128), lambda t, i, p: (0, 0, 0))] * 2
            + [
                pl.BlockSpec((1, 1, 2, height, 1024), lambda t, i, p: (system(t, p), 0, 0, i, 0)),
                pl.BlockSpec((1, 2, height, 256), lambda t, i, p: (system(t, p), 0, i, 0)),
            ],
            out_specs=[
                pl.BlockSpec(memory_space=pltpu.VMEM),
                pl.BlockSpec((1, 2, height, 256), lambda t, i, p: (system(t, p), 0, 0, 0)),
            ],
            scratch_shapes=[pltpu.VMEM((1024, 512), BF16)],
        ),
        out_shape=[
            pltpu.VMEM((2, 2, 3 * height, 256), F32),
            pltpu.HBM((2, 2, height, 256), F32),
        ],
        compiler_params=pltpu.CompilerParams(vmem_limit_bytes=TRAIL_VMEM),
        name="trail_first",
    )(place, mine, theirs, trail_factor, trail_rhs)


def take_blocks(place, received, blocks, tiles):
    for q in range(4):
        for row in range(8):
            value = received[q, :, 8 * row : 8 * row + 8, :].astype(F32).reshape(128, 128)
            blocks[128 * row : 128 * row + 128, 128 * q : 128 * q + 128] = value.astype(BF16)
        tiles[q] = received[q, :, 64:, :].astype(F32).reshape(128, 128).astype(BF16)
    near = pl.multiple_of(8 * place[2], 8)
    parts = [received[q, place[3], pl.ds(near, 8), :].astype(F32) for q in range(4)]
    pairs = [pair_lanes(parts[0], parts[1]), pair_lanes(parts[2], parts[3])]
    return [
        jnp.concatenate([pairs[0][part], pairs[1][part]], axis=1).astype(BF16) for part in range(2)
    ]


class Trail:
    scratch = staticmethod(
        lambda height: [
            pltpu.VMEM((4, 16, 72, 128), BF16),
            pltpu.VMEM((4, 2, height, 1024), BF16),
            pltpu.VMEM((2, height, 256), F32),
            pltpu.VMEM((4, 2, height, 256), BF16),
            pltpu.SemaphoreType.DMA((10,)),
        ]
    )

    def __init__(self, system, received, factor, near, far, out, scratch):
        arrived, rows, last, done, sems = scratch
        height = last.shape[1]
        self.system, self.near, self.height = system, near, height
        self.arrived, self.rows, self.last, self.done = arrived, rows, last, done
        copy = pltpu.make_async_copy
        self.take = copy(received, arrived, sems.at[0])
        self.take_last = copy(far.at[system], last, sems.at[1])
        self.take_rows = [
            copy(factor.at[system, 1, :, pl.ds(i * height, height)], rows.at[i], sems.at[2 + i])
            for i in range(4)
        ]
        self.give = [
            copy(done.at[i], out.at[system, :, pl.ds(i * height, height)], sems.at[6 + i])
            for i in range(4)
        ]

    def start(self):
        self.take.start()
        for one in self.take_rows:
            one.start()
        self.take_last.start()

    def run(self, blocks):
        height = self.height
        for i in range(4):
            self.take_rows[i].wait()
            real, imag = trail_product(self.rows[i].reshape(2 * height, 1024), blocks)
            if i < 3:
                cut = slice(i * height, i * height + height)
                before = (self.near[self.system, 0, cut, :], self.near[self.system, 1, cut, :])
            else:
                self.take_last.wait()
                before = (self.last[0], self.last[1])
            self.done[i, 0] = (before[0] - real).astype(BF16)
            self.done[i, 1] = (before[1] - imag).astype(BF16)
            self.give[i].start()

    def finish(self):
        for one in self.give:
            one.wait()


def trail_mine_kernel(place, received, factor, near, far, out, own, blocks, tiles, *scratch):
    trail = Trail(place[1], received, factor, near, far, out, scratch)
    trail.start()
    trail.take.wait()
    own[0], own[1] = take_blocks(place, trail.arrived, blocks, tiles)
    trail.run(blocks)
    trail.finish()


def trail_mine(place, received, trail_factor, near, far):
    height = far.shape[2]
    inside = pl.BlockSpec(memory_space=pltpu.VMEM)
    outside = pl.BlockSpec(memory_space=pltpu.HBM)
    return pl.pallas_call(
        trail_mine_kernel,
        in_specs=[pl.BlockSpec(memory_space=pltpu.SMEM), outside, outside, inside, outside],
        out_specs=[outside, inside, inside, inside],
        out_shape=[
            pltpu.HBM((2, 2, 4 * height, 256), BF16),
            pltpu.VMEM((2, 8, 256), BF16),
            pltpu.VMEM((1024, 512), BF16),
            pltpu.VMEM((4, 128, 128), BF16),
        ],
        scratch_shapes=Trail.scratch(height),
        compiler_params=pltpu.CompilerParams(vmem_limit_bytes=TRAIL_VMEM),
        name="trail_mine",
    )(place, received, trail_factor, near, far)


def trail_theirs_kernel(
    place, received, factor, near, far, mine, mine_tiles, own, first, before, spread, _, out, panel, gradient, blocks, tiles, *scratch
):
    core = place[1]
    trail = Trail(1 - core, received, factor, near, far, out, scratch)
    trail.start()
    panel[:, 0] = first[...]
    panel[core, 1] = own[...]
    trail.take.wait()
    real, imag = take_blocks(place, trail.arrived, blocks, tiles)
    panel[1 - core, 1, 0] = real
    panel[1 - core, 1, 1] = imag
    trail.run(blocks)
    slot_gradient(place, mine, blocks, (mine_tiles, tiles), before, spread, gradient)
    trail.finish()


def trail_theirs(place, received, trail_factor, near, far, mine, mine_tiles, own, first, before, spread, update):
    height = far.shape[2]
    inside = pl.BlockSpec(memory_space=pltpu.VMEM)
    outside = pl.BlockSpec(memory_space=pltpu.HBM)
    return pl.pallas_call(
        trail_theirs_kernel,
        in_specs=[pl.BlockSpec(memory_space=pltpu.SMEM), outside, outside, inside, outside]
        + [inside] * 6
        + [outside],
        out_specs=[outside, inside, inside],
        out_shape=[
            pltpu.HBM((2, 2, 4 * height, 256), BF16),
            jax.ShapeDtypeStruct((2, 2, 2, 8, 256), BF16),
            jax.ShapeDtypeStruct((3, 8), F32),
        ],
        scratch_shapes=[pltpu.VMEM((1024, 512), BF16), pltpu.VMEM((4, 128, 128), BF16)]
        + Trail.scratch(height),
        input_output_aliases={11: 0},
        compiler_params=pltpu.CompilerParams(vmem_limit_bytes=TRAIL_VMEM),
        name="trail_theirs",
    )(place, received, trail_factor, near, far, mine, mine_tiles, own, first, before, spread, update)


def spread_matrix():
    spread = np.zeros((128, 2, 3, 128), np.float32)
    for panel in range(2):
        for corner in range(3):
            for coordinate in range(3):
                lanes = slice(24 * corner + 8 * coordinate, 24 * corner + 8 * coordinate + 8)
                for part in range(2):
                    source = 18 * part + 9 * panel + 3 * corner + coordinate
                    for term in range(3):
                        spread[36 * term + source, panel, part, lanes] = 1.0
                spread[108 + 3 * panel + corner, panel, 2, lanes] = 32.0
                spread[114 + 3 * panel + corner, panel, 2, lanes] = 1.0
    return jnp.asarray(spread.reshape(128, 768), BF16)


def couple(mine, theirs):
    same = jnp.zeros((128, 128), F32)
    crossed = jnp.zeros((128, 128), F32)
    for near, far in zip(mine, theirs):
        near = near.astype(F32)
        far = far.astype(F32)
        same = same + near * far
        crossed = crossed + near * pltpu.roll(far, 64, 1)
    low = lanes_below((128, 128), 64)
    real = jnp.sum(jnp.where(low, same, -same), axis=1, keepdims=True)
    imag = jnp.sum(crossed, axis=1, keepdims=True)
    return real, imag


def couple_first_kernel(mine, theirs, out):
    low = lanes_below((128, 128), 64)
    for row in range(8):
        cut = slice(128 * row, 128 * row + 128)
        real, imag = couple([mine[q, cut, :] for q in range(4)], [theirs[q, cut, :] for q in range(4)])
        out[cut, :] = jnp.where(low, real, imag)


def couple_first(mine, theirs):
    return pl.pallas_call(
        couple_first_kernel,
        out_shape=pltpu.HBM((1024, 128), F32),
        compiler_params=pltpu.CompilerParams(vmem_limit_bytes=TRAIL_VMEM),
        name="couple_first",
    )(mine, theirs)


def slot_gradient(place, mine, theirs, tiles, before, spread, out):
    base = 8 * (16 * place[2] + place[3])
    target = (base + lax.rem(lax.broadcasted_iota(jnp.int32, (128, 128), 1), 8)).astype(F32)
    total = jnp.zeros((8, 128), F32)
    for source in range(4):
        for side in range(2):
            row = 2 * source + (place[1] if side == 0 else 1 - place[1])
            cut = pl.ds(pl.multiple_of(128 * row, 128), 128)
            lanes = [slice(128 * q, 128 * q + 128) for q in range(4)]
            real, imag = couple([mine[cut, q] for q in lanes], [theirs[cut, q] for q in lanes])
            first = before[cut, :]
            table = jnp.dot(tiles[side][source], spread[...], preferred_element_type=F32)
            for at, real, imag in ((0, first[:, :1], first[:, 64:65]), (384, real, imag)):
                value = table[:, at + 128 : at + 256] * imag - table[:, at : at + 128] * real
                value = jnp.where(table[:, at + 256 : at + 384] == target, value, 0.0)
                total = total + jnp.sum(value.reshape(16, 8, 128), axis=0)
    total = jnp.sum(total, axis=0, keepdims=True)
    total = total + pltpu.roll(total, 104, 1) + pltpu.roll(total, 80, 1)
    for coordinate in range(3):
        out[coordinate : coordinate + 1, :] = total[:, 8 * coordinate : 8 * coordinate + 8]


def rounds_x(value):
    sent = [lax.ppermute(value, "x", [(i, (i + step) % 4) for i in range(4)]) for step in (1, 2, 3)]
    return [value, *sent]


def swap_core(value):
    return lax.ppermute(value, "core", [(0, 1), (1, 0)])


def element_tile(shape_tiles, element_vertices, vertex_slot):
    values = shape_tiles.transpose(3, 0, 2, 1).reshape(8, 36)
    high = lax.reduce_precision(values, 8, 7)
    rest = values - high
    mid = lax.reduce_precision(rest, 8, 7)
    low = rest - mid
    slots = vertex_slot[element_vertices].transpose(1, 0, 2).reshape(8, 6)
    parts = [high, mid, low, (slots // 32).astype(F32), (slots % 32).astype(F32), jnp.zeros((8, 8), F32)]
    return jnp.concatenate(parts, axis=1).astype(BF16)


def steps(
    panel_inverse,
    panel_below,
    trail_factor,
    first_rhs,
    second_rhs,
    trail_rhs,
    shape_tiles,
    element_vertices,
    vertex_slot,
):
    x = lax.axis_index("x")
    core = lax.axis_index("core")
    col = lax.axis_index("col")
    outside = lambda value: pltpu.with_memory_space_constraint(value, pltpu.HBM)
    trail_factor, panel_inverse, first_rhs = map(outside, (trail_factor, panel_inverse, first_rhs))
    panel_below, second_rhs = map(outside, (panel_below, second_rhs))
    place = jnp.stack([x, core, 2 * x + core, col]).astype(jnp.int32)

    first, send, own, give = prepare(panel_inverse, first_rhs, panel_below, second_rhs)
    received = lax.all_to_all(send.reshape(128, 2, 8, 128), ALL, 0, 0, tiled=True)

    other = swap_core(give)
    chip = jnp.where(core == 0, jnp.stack([own, other]), jnp.stack([other, own]))
    rows = rounds_x(chip)
    tile = element_tile(shape_tiles, element_vertices, vertex_slot)

    first_block, send = right_side(place, received, rows)
    received = lax.all_to_all(send, "col", 0, 0, tiled=True)
    first_mine = rounds_x(first_block)
    first_mine = jnp.stack(first_mine)
    first_theirs = swap_core(first_mine)

    send = second_rows(place, received, rows, tile)
    second_mine = lax.all_to_all(send, ("x", "col"), 0, 0, tiled=True)

    near, far = trail_first(place, first_mine, first_theirs, trail_factor, outside(trail_rhs))
    far = outside(far)
    before = couple_first(first_mine, first_theirs)

    second_theirs = swap_core(second_mine)
    mine = second_mine.reshape(4, 16, 72, 128)
    theirs = second_theirs.reshape(4, 16, 72, 128)
    update, own, mine, mine_tiles = trail_mine(place, mine, trail_factor, near, far)
    update, panel_solution, gradient = trail_theirs(
        place,
        theirs,
        trail_factor,
        near,
        far,
        mine,
        mine_tiles,
        own,
        first,
        before,
        spread_matrix(),
        update,
    )
    return (panel_solution, update, gradient)


def solution(mesh):
    fine = Mesh(mesh.devices.reshape(4, 2, 16), ALL)
    return jax.shard_map(
        steps,
        mesh=fine,
        in_specs=(
            P(None, None, None, ALL, None),
            P(None, None, ALL, None),
            P(None, None, None, ALL, None),
            P(),
            P(None, None, ALL, None),
            P(None, None, ALL, None),
            P(None, None, None, ALL),
            P(None, ALL, None),
            P(),
        ),
        out_specs=(
            P(None, None, None, ALL, None),
            P(None, None, ALL, None),
            P(None, ALL),
        ),
        check_vma=False,
    )
```

```python
import jax
import jax.numpy as jnp
import numpy as np
from jax import lax
from jax.experimental import pallas as pl
from jax.experimental.pallas import tpu as pltpu
from jax.sharding import Mesh
from jax.sharding import PartitionSpec as P


ALL = ("x", "core", "col")
F32 = jnp.float32
BF16 = jnp.bfloat16
SMALL_VMEM = 12 * 1024 * 1024
SPACE = pltpu.VMEM


def lanes_below(shape, bound):
    return lax.broadcasted_iota(jnp.int32, shape, len(shape) - 1) < bound


def pair_lanes(left, right):
    low = lanes_below(left.shape, 64)
    real = jnp.where(low, left, pltpu.roll(right, 64, 1))
    imag = jnp.where(low, pltpu.roll(left, 64, 1), right)
    return real, imag


def fold_parts(top, low):
    turned = pltpu.roll(low, 64, 1)
    return top + jnp.where(lanes_below(low.shape, 64), -turned, turned)


def prepare_kernel(inverse, rhs, below, own_rhs, first, send, own, give):
    system = pl.program_id(0)
    core = lax.axis_index("core")
    left = jnp.concatenate([inverse[0, 0, 0].astype(F32), inverse[0, 0, 1].astype(F32)]).astype(BF16)
    by_real = jnp.dot(left, rhs[0, 0], preferred_element_type=F32)
    by_imag = jnp.dot(left, rhs[0, 1], preferred_element_type=F32)
    real = (by_real[:8] - by_imag[8:]).astype(BF16)
    imag = (by_imag[:8] + by_real[8:]).astype(BF16)
    first[0, 0] = real
    first[0, 1] = imag
    real = real.astype(F32)
    imag = imag.astype(F32)
    for half in range(2):
        cut = slice(128 * half, 128 * half + 128)
        even, odd = pair_lanes(real[:, cut], imag[:, cut])
        for group, value in ((2 * half, even), (2 * half + 1, odd)):
            value = value.astype(BF16)
            for col in range(16):
                send[group, 0, col, 0] = value
    lane_block = lax.broadcasted_iota(jnp.int32, (8, 128), 1) // 8
    pieces = [
        below[0, part, :, 128 * row : 128 * row + 128].astype(F32)
        for part in range(2)
        for row in range(8)
    ]
    for col in range(16):
        value = pltpu.roll(pieces[0], (128 - 8 * col) % 128, 1)
        for block in range(1, 16):
            turned = pltpu.roll(pieces[block], (8 * block - 8 * col) % 128, 1)
            value = jnp.where(lane_block == block, turned, value)
        value = value.astype(BF16)
        for group in range(4):
            send[group, 0, col, 1] = value

    def fill(target):
        for part in range(2):
            target[part, :, :1024] = inverse[0, 1, part]
            target[part, :, 1024:] = own_rhs[0, part]

    @pl.when(system == core)
    def _():
        fill(own)

    @pl.when(system != core)
    def _():
        fill(give)


def prepare(panel_inverse, first_rhs, panel_below, second_rhs):
    return pl.pallas_call(
        prepare_kernel,
        grid=(2,),
        in_specs=[
            pl.BlockSpec((1, 2, 2, 8, 1024), lambda s: (s, 0, 0, 0, 0)),
            pl.BlockSpec((1, 2, 1024, 256), lambda s: (s, 0, 0, 0)),
            pl.BlockSpec((1, 2, 8, 1024), lambda s: (s, 0, 0, 0)),
            pl.BlockSpec((1, 2, 8, 256), lambda s: (s, 0, 0, 0)),
        ],
        out_specs=[
            pl.BlockSpec((1, 2, 8, 256), lambda s: (s, 0, 0, 0)),
            pl.BlockSpec((4, 1, 16, 2, 8, 128), lambda s: (0, s, 0, 0, 0, 0)),
            pl.BlockSpec((2, 8, 1280), lambda s: (0, 0, 0)),
            pl.BlockSpec((2, 8, 1280), lambda s: (0, 0, 0)),
        ],
        out_shape=[
            jax.ShapeDtypeStruct((2, 2, 8, 256), BF16),
            jax.ShapeDtypeStruct((4, 2, 16, 2, 8, 128), BF16),
            jax.ShapeDtypeStruct((2, 8, 1280), BF16),
            jax.ShapeDtypeStruct((2, 8, 1280), BF16),
        ],
        compiler_params=pltpu.CompilerParams(vmem_limit_bytes=SMALL_VMEM),
        name="prepare",
    )(panel_inverse, first_rhs, panel_below, second_rhs)


def right_kernel(place, received, rows0, rows1, rows2, rows3, block, send, offset):
    x = place[0]
    half = pl.multiple_of(1024 + 128 * (x // 2), 128)
    odd = x % 2 == 1
    for step, rows in enumerate((rows0, rows1, rows2, rows3)):
        source = lax.rem(x - step + 4, 4)
        for core in range(2):
            real = rows[core, 0, :, pl.ds(half, 128)].astype(F32)
            imag = rows[core, 1, :, pl.ds(half, 128)].astype(F32)
            even_pair, odd_pair = pair_lanes(real, imag)
            value = jnp.where(odd, odd_pair, even_pair)
            offset[pl.ds(pl.multiple_of(16 * source + 8 * core, 8), 8), :] = value
    first = received[:, 0].astype(F32).reshape(1024, 128).astype(BF16)
    below = received[:, 1].astype(F32).reshape(1024, 128).astype(BF16)
    block[...] = first
    product = lax.dot_general(below, first, (((0,), (0,)), ((), ())), preferred_element_type=F32)
    right = (offset[...] - fold_parts(product[:64], product[64:])).astype(BF16)
    for col in range(16):
        send[col] = right


def right_side(place, received, rows):
    inside = pl.BlockSpec(memory_space=pltpu.VMEM)
    return pl.pallas_call(
        right_kernel,
        in_specs=[pl.BlockSpec(memory_space=pltpu.SMEM)] + [inside] * 5,
        out_specs=[inside] * 2,
        out_shape=[SPACE((1024, 128), BF16), SPACE((16, 64, 128), BF16)],
        scratch_shapes=[pltpu.VMEM((64, 128), F32)],
        compiler_params=pltpu.CompilerParams(vmem_limit_bytes=SMALL_VMEM),
        name="right_side",
    )(place, received, *rows)


def second_kernel(place, received, rows0, rows1, rows2, rows3, tile, send):
    x = place[0]
    right = received[...].astype(F32).reshape(16, 8, 8, 128)
    right = right.transpose(1, 0, 2, 3).reshape(1024, 128).astype(BF16)
    pieces = [
        rows[core, part, :, :1024].astype(F32)
        for part in range(2)
        for rows in (rows0, rows1, rows2, rows3)
        for core in range(2)
    ]
    left = jnp.concatenate(pieces).astype(BF16)
    product = jnp.dot(left, right, preferred_element_type=F32)
    value = fold_parts(product[:64], product[64:]).astype(BF16)
    for step in range(4):
        target = pl.multiple_of(16 * lax.rem(x - step + 4, 4), 16)
        part = value[16 * step : 16 * step + 16]
        for copy in range(64):
            send[copy, pl.ds(target, 16), :] = part
    for copy in range(64):
        send[copy, 64:] = tile[...]


def second_rows(place, received, rows, tile):
    inside = pl.BlockSpec(memory_space=pltpu.VMEM)
    return pl.pallas_call(
        second_kernel,
        in_specs=[pl.BlockSpec(memory_space=pltpu.SMEM)] + [inside] * 6,
        out_specs=inside,
        out_shape=SPACE((64, 72, 128), BF16),
        compiler_params=pltpu.CompilerParams(vmem_limit_bytes=SMALL_VMEM),
        name="second_rows",
    )(place, received, *rows, tile)


def set_blocks(blocks, at, parts):
    for half in range(2):
        real, imag = pair_lanes(parts[2 * half], parts[2 * half + 1])
        blocks[at : at + 128, 128 * half : 128 * half + 128] = real.astype(BF16)
        blocks[at : at + 128, 256 + 128 * half : 384 + 128 * half] = imag.astype(BF16)


def trail_product(stacked, blocks):
    height = stacked.shape[0] // 2
    product = jnp.dot(stacked, blocks[...], preferred_element_type=F32)
    top, low = product[:height], product[height:]
    return top[:, :256] - low[:, 256:], top[:, 256:] + low[:, :256]


def trail_first_kernel(place, mine, theirs, factor, rhs, total, before, early, blocks, rows, start, done, sems):
    x, core = place[0], place[1]
    height = rows.shape[3]
    copy = pltpu.make_async_copy
    cuts = [pl.ds(i * height, height) for i in range(4)]
    systems = (core, 1 - core)
    take = [
        [
            *(copy(factor.at[systems[t], 0, :, cuts[i]], rows.at[t, i], sems.at[t, i]) for i in range(4)),
            copy(rhs.at[systems[t]], start.at[t], sems.at[t, 4]),
        ]
        for t in range(2)
    ]
    give = [copy(done.at[t], total.at[systems[t]], sems.at[t, 5]) for t in range(2)]
    take_early = [copy(factor.at[core, 1, :, cuts[i]], early.at[i], sems.at[2, i]) for i in range(2)]
    for one in (*take[0], *take[1], *take_early):
        one.start()
    for t, source in enumerate((mine, theirs)):
        for row in range(8):
            cut = slice(128 * row, 128 * row + 128)
            parts = [source[lax.rem(x - q + 4, 4), cut, :].astype(F32) for q in range(4)]
            set_blocks(blocks.at[t], 128 * row, parts)
    for t in range(2):
        for one in take[t]:
            one.wait()
        for i in range(4):
            real, imag = trail_product(rows[t, i].reshape(2 * height, 1024), blocks.at[t])
            cut = slice(i * height, i * height + height)
            done[t, 0, cut, :] = start[t, 0, cut, :].astype(F32) - real
            done[t, 1, cut, :] = start[t, 1, cut, :].astype(F32) - imag
        give[t].start()
    low = lanes_below((128, 128), 64)
    for row in range(8):
        cut = slice(128 * row, 128 * row + 128)
        real, imag = couple(blocks[0, cut, :], blocks[1, cut, :])
        before[cut, :] = jnp.where(low, real, imag)
    for one in (*take_early, *give):
        one.wait()


def trail_first(place, mine, theirs, trail_factor, trail_rhs):
    rows = trail_rhs.shape[2]
    height = rows // 4
    inside = pl.BlockSpec(memory_space=pltpu.VMEM)
    outside = pl.BlockSpec(memory_space=pltpu.HBM)
    return pl.pallas_call(
        trail_first_kernel,
        in_specs=[pl.BlockSpec(memory_space=pltpu.SMEM), inside, inside, outside, outside],
        out_specs=[outside, inside, inside],
        out_shape=[
            pltpu.HBM((2, 2, rows, 256), F32),
            pltpu.HBM((1024, 128), F32),
            pltpu.VMEM((2, 2, height, 1024), BF16),
        ],
        scratch_shapes=[
            pltpu.VMEM((2, 1024, 512), BF16),
            pltpu.VMEM((2, 4, 2, height, 1024), BF16),
            pltpu.VMEM((2, 2, rows, 256), BF16),
            pltpu.VMEM((2, 2, rows, 256), F32),
            pltpu.SemaphoreType.DMA((3, 6)),
        ],
        compiler_params=pltpu.CompilerParams(vmem_limit_bytes=28 * 1024 * 1024),
        name="trail_first",
    )(place, mine, theirs, trail_factor, trail_rhs)


def take_blocks(place, received, blocks, tiles):
    for row in range(8):
        parts = [
            received[q, :, 8 * row : 8 * row + 8, :].astype(F32).reshape(128, 128) for q in range(4)
        ]
        set_blocks(blocks, 128 * row, parts)
    for q in range(4):
        tiles[q] = received[q, :, 64:, :].astype(F32).reshape(128, 128).astype(BF16)
    near = pl.multiple_of(8 * place[2], 8)
    parts = [received[q, place[3], pl.ds(near, 8), :].astype(F32) for q in range(4)]
    pairs = [pair_lanes(parts[0], parts[1]), pair_lanes(parts[2], parts[3])]
    return [
        jnp.concatenate([pairs[0][part], pairs[1][part]], axis=1).astype(BF16) for part in range(2)
    ]


def finish_rows(i, product, before, done):
    height = done.shape[2]
    cut = slice(i * height, i * height + height)
    done[i, 0] = (before[0, cut, :] - product[0]).astype(BF16)
    done[i, 1] = (before[1, cut, :] - product[1]).astype(BF16)


def trail_mine_kernel(
    place, received, factor, early, total, out, own, blocks, tiles, later, rest, arrived, rows, before, done, sems
):
    core = place[1]
    height = rows.shape[1] // 2
    copy = pltpu.make_async_copy
    cuts = [pl.ds(i * height, height) for i in range(4)]
    take = copy(received, arrived, sems.at[0])
    take_row = copy(factor.at[core, 1, :, pl.ds(2 * height, 2 * height)], rows, sems.at[1])
    take_before = copy(total.at[core], before, sems.at[2])
    take_rest = copy(total.at[1 - core], rest, sems.at[3])
    give = [copy(done.at[i], out.at[core, :, cuts[i]], sems.at[4 + i]) for i in range(4)]
    take_later = [
        copy(factor.at[1 - core, 1, :, cuts[i]], later.at[i], sems.at[8 + i]) for i in range(4)
    ]
    take.start()
    take.wait()
    for one in (take_row, take_before, *take_later, take_rest):
        one.start()
    own[0], own[1] = take_blocks(place, arrived, blocks, tiles)
    products = [trail_product(early[i].reshape(2 * height, 1024), blocks) for i in range(2)]
    take_row.wait()
    take_before.wait()
    for i in range(2):
        cut = slice(i * height, i * height + height)
        products.append(trail_product(rows[:, cut, :].reshape(2 * height, 1024), blocks))
    for i in range(4):
        finish_rows(i, products[i], before, done)
        give[i].start()
    for one in (*take_later, take_rest, *give):
        one.wait()


def trail_mine(place, received, trail_factor, early, total):
    rows = total.shape[2]
    height = rows // 4
    inside = pl.BlockSpec(memory_space=pltpu.VMEM)
    outside = pl.BlockSpec(memory_space=pltpu.HBM)
    return pl.pallas_call(
        trail_mine_kernel,
        in_specs=[pl.BlockSpec(memory_space=pltpu.SMEM), outside, outside, inside, outside],
        out_specs=[outside] + [inside] * 5,
        out_shape=[
            pltpu.HBM((2, 2, rows, 256), BF16),
            pltpu.VMEM((2, 8, 256), BF16),
            pltpu.VMEM((1024, 512), BF16),
            pltpu.VMEM((4, 128, 128), BF16),
            pltpu.VMEM((4, 2, height, 1024), BF16),
            pltpu.VMEM((2, rows, 256), F32),
        ],
        scratch_shapes=[
            pltpu.VMEM((4, 16, 72, 128), BF16),
            pltpu.VMEM((2, 2 * height, 1024), BF16),
            pltpu.VMEM((2, rows, 256), F32),
            pltpu.VMEM((4, 2, height, 256), BF16),
            pltpu.SemaphoreType.DMA((12,)),
        ],
        compiler_params=pltpu.CompilerParams(vmem_limit_bytes=14 * 1024 * 1024),
        name="trail_mine",
    )(place, received, trail_factor, early, total)


def trail_theirs_kernel(
    place, received, rows, rest, mine, mine_tiles, own, first, before, spread, _, out, panel, gradient, blocks, tiles, done, sems
):
    core = place[1]
    height = rows.shape[2]
    give = [
        pltpu.make_async_copy(
            done.at[i], out.at[1 - core, :, pl.ds(i * height, height)], sems.at[i]
        )
        for i in range(4)
    ]
    panel[:, 0] = first[...]
    panel[core, 1] = own[...]
    real, imag = take_blocks(place, received, blocks, tiles)
    panel[1 - core, 1, 0] = real
    panel[1 - core, 1, 1] = imag
    for i in range(4):
        product = trail_product(rows[i].reshape(2 * height, 1024), blocks)
        finish_rows(i, product, rest, done)
        give[i].start()
    slot_gradient(place, mine, blocks, (mine_tiles, tiles), before, spread, gradient)
    for one in give:
        one.wait()


def trail_theirs(place, received, later, rest, mine, mine_tiles, own, first, before, spread, update):
    height = later.shape[2]
    inside = pl.BlockSpec(memory_space=pltpu.VMEM)
    outside = pl.BlockSpec(memory_space=pltpu.HBM)
    return pl.pallas_call(
        trail_theirs_kernel,
        in_specs=[pl.BlockSpec(memory_space=pltpu.SMEM)] + [inside] * 9 + [outside],
        out_specs=[outside, inside, inside],
        out_shape=[
            pltpu.HBM(update.shape, BF16),
            jax.ShapeDtypeStruct((2, 2, 2, 8, 256), BF16),
            jax.ShapeDtypeStruct((3, 8), F32),
        ],
        scratch_shapes=[
            pltpu.VMEM((1024, 512), BF16),
            pltpu.VMEM((4, 128, 128), BF16),
            pltpu.VMEM((4, 2, height, 256), BF16),
            pltpu.SemaphoreType.DMA((4,)),
        ],
        input_output_aliases={10: 0},
        compiler_params=pltpu.CompilerParams(vmem_limit_bytes=14 * 1024 * 1024),
        name="trail_theirs",
    )(place, received, later, rest, mine, mine_tiles, own, first, before, spread, update)


def spread_matrix():
    spread = np.zeros((128, 2, 3, 128), np.float32)
    for panel in range(2):
        for corner in range(3):
            for coordinate in range(3):
                lanes = slice(24 * corner + 8 * coordinate, 24 * corner + 8 * coordinate + 8)
                for part in range(2):
                    source = 18 * part + 9 * panel + 3 * corner + coordinate
                    for term in range(3):
                        spread[36 * term + source, panel, part, lanes] = 1.0
                spread[108 + 3 * panel + corner, panel, 2, lanes] = 32.0
                spread[114 + 3 * panel + corner, panel, 2, lanes] = 1.0
    return jnp.asarray(spread.reshape(128, 768), BF16)


def couple(near, far):
    near = near.astype(F32)
    far = far.astype(F32)
    near_real, near_imag, far_real, far_imag = near[:, :256], near[:, 256:], far[:, :256], far[:, 256:]
    real = near_real * far_real - near_imag * far_imag
    imag = near_real * far_imag + near_imag * far_real
    sums = jnp.concatenate([real[:, :128] + real[:, 128:], imag[:, :128] + imag[:, 128:]])
    sums = jnp.broadcast_to(jnp.sum(sums, axis=1, keepdims=True), (256, 128))
    return sums[:128], sums[128:]


def slot_gradient(place, mine, theirs, tiles, before, spread, out):
    base = 8 * (16 * place[2] + place[3])
    target = (base + lax.rem(lax.broadcasted_iota(jnp.int32, (128, 128), 1), 8)).astype(F32)
    source_lane = lax.broadcasted_iota(jnp.int32, (128, 256), 0)
    high = lax.broadcasted_iota(jnp.int32, (128, 256), 1) >= 128
    pick = (source_lane == jnp.where(high, 64, 0)).astype(F32)
    total = jnp.zeros((8, 128), F32)
    for source in range(4):
        for side in range(2):
            row = 2 * source + (place[1] if side == 0 else 1 - place[1])
            cut = pl.ds(pl.multiple_of(128 * row, 128), 128)
            value = before[cut, :]
            first = jnp.concatenate([jnp.broadcast_to(value[:, :1], (128, 128)), jnp.broadcast_to(value[:, 64:65], (128, 128))], axis=1)
            second = couple(mine[cut, :], theirs[cut, :])
            table = jnp.dot(tiles[side][source], spread[...], preferred_element_type=F32)
            for at, real, imag in ((0, first[:, :128], first[:, 128:]), (384, *second)):
                value = table[:, at + 128 : at + 256] * imag - table[:, at : at + 128] * real
                value = jnp.where(table[:, at + 256 : at + 384] == target, value, 0.0)
                total = total + jnp.sum(value.reshape(16, 8, 128), axis=0)
    total = jnp.sum(total, axis=0, keepdims=True)
    total = total + pltpu.roll(total, 104, 1) + pltpu.roll(total, 80, 1)
    for coordinate in range(3):
        out[coordinate : coordinate + 1, :] = total[:, 8 * coordinate : 8 * coordinate + 8]


def rounds_x(value):
    sent = [lax.ppermute(value, "x", [(i, (i + step) % 4) for i in range(4)]) for step in (1, 2, 3)]
    return [value, *sent]


def swap_core(value):
    return lax.ppermute(value, "core", [(0, 1), (1, 0)])


def element_tile(shape_tiles, element_vertices, vertex_slot):
    values = shape_tiles.transpose(3, 0, 2, 1).reshape(8, 36)
    high = lax.reduce_precision(values, 8, 7)
    rest = values - high
    mid = lax.reduce_precision(rest, 8, 7)
    low = rest - mid
    slots = vertex_slot[element_vertices].transpose(1, 0, 2).reshape(8, 6)
    parts = [high, mid, low, (slots // 32).astype(F32), (slots % 32).astype(F32), jnp.zeros((8, 8), F32)]
    return jnp.concatenate(parts, axis=1).astype(BF16)


def steps(
    panel_inverse,
    panel_below,
    trail_factor,
    first_rhs,
    second_rhs,
    trail_rhs,
    shape_tiles,
    element_vertices,
    vertex_slot,
):
    x = lax.axis_index("x")
    core = lax.axis_index("core")
    col = lax.axis_index("col")
    outside = lambda value: pltpu.with_memory_space_constraint(value, pltpu.HBM)
    trail_factor, panel_inverse, first_rhs = map(outside, (trail_factor, panel_inverse, first_rhs))
    panel_below, second_rhs = map(outside, (panel_below, second_rhs))
    place = jnp.stack([x, core, 2 * x + core, col]).astype(jnp.int32)

    first, send, own, give = prepare(panel_inverse, first_rhs, panel_below, second_rhs)
    received = lax.all_to_all(send.reshape(128, 2, 8, 128), ALL, 0, 0, tiled=True)

    other = swap_core(give)
    chip = jnp.where(core == 0, jnp.stack([own, other]), jnp.stack([other, own]))
    rows = rounds_x(chip)
    tile = element_tile(shape_tiles, element_vertices, vertex_slot)

    first_block, send = right_side(place, received, rows)
    received = lax.all_to_all(send, "col", 0, 0, tiled=True)
    first_mine = rounds_x(first_block)
    first_mine = jnp.stack(first_mine)
    first_theirs = swap_core(first_mine)

    send = second_rows(place, received, rows, tile)
    second_mine = lax.all_to_all(send, ("x", "col"), 0, 0, tiled=True)

    total, before, early = trail_first(
        place, first_mine, first_theirs, trail_factor, outside(trail_rhs)
    )
    total = outside(total)

    second_theirs = swap_core(second_mine)
    mine = second_mine.reshape(4, 16, 72, 128)
    theirs = second_theirs.reshape(4, 16, 72, 128)
    update, own, mine, mine_tiles, later, rest = trail_mine(place, mine, trail_factor, early, total)
    update, panel_solution, gradient = trail_theirs(
        place,
        theirs,
        later,
        rest,
        mine,
        mine_tiles,
        own,
        first,
        before,
        spread_matrix(),
        update,
    )
    return (panel_solution, update, gradient)


def solution(mesh):
    fine = Mesh(mesh.devices.reshape(4, 2, 16), ALL)
    return jax.shard_map(
        steps,
        mesh=fine,
        in_specs=(
            P(None, None, None, ALL, None),
            P(None, None, ALL, None),
            P(None, None, None, ALL, None),
            P(),
            P(None, None, ALL, None),
            P(None, None, ALL, None),
            P(None, None, None, ALL),
            P(None, ALL, None),
            P(),
        ),
        out_specs=(
            P(None, None, None, ALL, None),
            P(None, None, ALL, None),
            P(None, ALL),
        ),
        check_vma=False,
    )
```

```python
import jax
import jax.numpy as jnp
import numpy as np
from jax import lax
from jax.experimental import pallas as pl
from jax.experimental.pallas import tpu as pltpu
from jax.sharding import Mesh
from jax.sharding import PartitionSpec as P


ALL = ("x", "core", "col")
F32 = jnp.float32
BF16 = jnp.bfloat16
SMALL_VMEM = 12 * 1024 * 1024
SPACE = pltpu.VMEM


def lanes_below(shape, bound):
    return lax.broadcasted_iota(jnp.int32, shape, len(shape) - 1) < bound


def pair_lanes(left, right):
    low = lanes_below(left.shape, 64)
    real = jnp.where(low, left, pltpu.roll(right, 64, 1))
    imag = jnp.where(low, pltpu.roll(left, 64, 1), right)
    return real, imag


def fold_parts(top, low):
    turned = pltpu.roll(low, 64, 1)
    return top + jnp.where(lanes_below(low.shape, 64), -turned, turned)


def prepare_kernel(inverse, rhs, below, own_rhs, first, send, own, give):
    system = pl.program_id(0)
    core = lax.axis_index("core")
    left = jnp.concatenate([inverse[0, 0, 0].astype(F32), inverse[0, 0, 1].astype(F32)]).astype(BF16)
    by_real = jnp.dot(left, rhs[0, 0], preferred_element_type=F32)
    by_imag = jnp.dot(left, rhs[0, 1], preferred_element_type=F32)
    real = (by_real[:8] - by_imag[8:]).astype(BF16)
    imag = (by_imag[:8] + by_real[8:]).astype(BF16)
    first[0, 0] = real
    first[0, 1] = imag
    real = real.astype(F32)
    imag = imag.astype(F32)
    for half in range(2):
        cut = slice(128 * half, 128 * half + 128)
        even, odd = pair_lanes(real[:, cut], imag[:, cut])
        for group, value in ((2 * half, even), (2 * half + 1, odd)):
            value = value.astype(BF16)
            for col in range(16):
                send[group, 0, col, 0] = value
    lane_block = lax.broadcasted_iota(jnp.int32, (8, 128), 1) // 8
    pieces = [
        below[0, part, :, 128 * row : 128 * row + 128].astype(F32)
        for part in range(2)
        for row in range(8)
    ]
    for col in range(16):
        value = pltpu.roll(pieces[0], (128 - 8 * col) % 128, 1)
        for block in range(1, 16):
            turned = pltpu.roll(pieces[block], (8 * block - 8 * col) % 128, 1)
            value = jnp.where(lane_block == block, turned, value)
        value = value.astype(BF16)
        for group in range(4):
            send[group, 0, col, 1] = value

    def fill(target):
        for part in range(2):
            target[part, :, :1024] = inverse[0, 1, part]
            target[part, :, 1024:] = own_rhs[0, part]

    @pl.when(system == core)
    def _():
        fill(own)

    @pl.when(system != core)
    def _():
        fill(give)


def prepare(panel_inverse, first_rhs, panel_below, second_rhs):
    return pl.pallas_call(
        prepare_kernel,
        grid=(2,),
        in_specs=[
            pl.BlockSpec((1, 2, 2, 8, 1024), lambda s: (s, 0, 0, 0, 0)),
            pl.BlockSpec((1, 2, 1024, 256), lambda s: (s, 0, 0, 0)),
            pl.BlockSpec((1, 2, 8, 1024), lambda s: (s, 0, 0, 0)),
            pl.BlockSpec((1, 2, 8, 256), lambda s: (s, 0, 0, 0)),
        ],
        out_specs=[
            pl.BlockSpec((1, 2, 8, 256), lambda s: (s, 0, 0, 0)),
            pl.BlockSpec((4, 1, 16, 2, 8, 128), lambda s: (0, s, 0, 0, 0, 0)),
            pl.BlockSpec((2, 8, 1280), lambda s: (0, 0, 0)),
            pl.BlockSpec((2, 8, 1280), lambda s: (0, 0, 0)),
        ],
        out_shape=[
            jax.ShapeDtypeStruct((2, 2, 8, 256), BF16),
            jax.ShapeDtypeStruct((4, 2, 16, 2, 8, 128), BF16),
            jax.ShapeDtypeStruct((2, 8, 1280), BF16),
            jax.ShapeDtypeStruct((2, 8, 1280), BF16),
        ],
        compiler_params=pltpu.CompilerParams(vmem_limit_bytes=SMALL_VMEM),
        name="prepare",
    )(panel_inverse, first_rhs, panel_below, second_rhs)


def right_kernel(place, received, rows0, rows1, rows2, rows3, block, send, offset):
    x = place[0]
    half = pl.multiple_of(1024 + 128 * (x // 2), 128)
    odd = x % 2 == 1
    for step, rows in enumerate((rows0, rows1, rows2, rows3)):
        source = lax.rem(x - step + 4, 4)
        for core in range(2):
            real = rows[core, 0, :, pl.ds(half, 128)].astype(F32)
            imag = rows[core, 1, :, pl.ds(half, 128)].astype(F32)
            even_pair, odd_pair = pair_lanes(real, imag)
            value = jnp.where(odd, odd_pair, even_pair)
            offset[pl.ds(pl.multiple_of(16 * source + 8 * core, 8), 8), :] = value
    first = received[:, 0].astype(F32).reshape(1024, 128).astype(BF16)
    below = received[:, 1].astype(F32).reshape(1024, 128).astype(BF16)
    block[...] = first
    product = lax.dot_general(below, first, (((0,), (0,)), ((), ())), preferred_element_type=F32)
    right = (offset[...] - fold_parts(product[:64], product[64:])).astype(BF16)
    for col in range(16):
        send[col] = right


def right_side(place, received, rows):
    inside = pl.BlockSpec(memory_space=pltpu.VMEM)
    return pl.pallas_call(
        right_kernel,
        in_specs=[pl.BlockSpec(memory_space=pltpu.SMEM)] + [inside] * 5,
        out_specs=[inside] * 2,
        out_shape=[SPACE((1024, 128), BF16), SPACE((16, 64, 128), BF16)],
        scratch_shapes=[pltpu.VMEM((64, 128), F32)],
        compiler_params=pltpu.CompilerParams(vmem_limit_bytes=SMALL_VMEM),
        name="right_side",
    )(place, received, *rows)


def second_kernel(place, received, rows0, rows1, rows2, rows3, tile, send):
    x = place[0]
    right = received[...].astype(F32).reshape(16, 8, 8, 128)
    right = right.transpose(1, 0, 2, 3).reshape(1024, 128).astype(BF16)
    pieces = [
        rows[core, part, :, :1024].astype(F32)
        for part in range(2)
        for rows in (rows0, rows1, rows2, rows3)
        for core in range(2)
    ]
    left = jnp.concatenate(pieces).astype(BF16)
    product = jnp.dot(left, right, preferred_element_type=F32)
    value = fold_parts(product[:64], product[64:]).astype(BF16)
    for step in range(4):
        target = pl.multiple_of(16 * lax.rem(x - step + 4, 4), 16)
        part = value[16 * step : 16 * step + 16]
        for copy in range(64):
            send[copy, pl.ds(target, 16), :] = part
    for copy in range(64):
        send[copy, 64:] = tile[...]


def second_rows(place, received, rows, tile):
    inside = pl.BlockSpec(memory_space=pltpu.VMEM)
    return pl.pallas_call(
        second_kernel,
        in_specs=[pl.BlockSpec(memory_space=pltpu.SMEM)] + [inside] * 6,
        out_specs=inside,
        out_shape=SPACE((64, 72, 128), BF16),
        compiler_params=pltpu.CompilerParams(vmem_limit_bytes=SMALL_VMEM),
        name="second_rows",
    )(place, received, *rows, tile)


def set_blocks(blocks, at, parts):
    for half in range(2):
        real, imag = pair_lanes(parts[2 * half], parts[2 * half + 1])
        blocks[at : at + 128, 128 * half : 128 * half + 128] = real.astype(BF16)
        blocks[at : at + 128, 256 + 128 * half : 384 + 128 * half] = imag.astype(BF16)


def trail_product(stacked, blocks):
    height = stacked.shape[0] // 2
    product = jnp.dot(stacked, blocks[...], preferred_element_type=F32)
    top, low = product[:height], product[height:]
    return top[:, :256] - low[:, 256:], top[:, 256:] + low[:, :256]


def trail_first_kernel(place, mine, theirs, factor, rhs, total, before, early, blocks, rows, start, done, sems):
    x, core = place[0], place[1]
    height = rows.shape[3]
    copy = pltpu.make_async_copy
    cuts = [pl.ds(i * height, height) for i in range(4)]
    systems = (core, 1 - core)
    take = [
        [
            *(copy(factor.at[systems[t], 0, :, cuts[i]], rows.at[t, i], sems.at[t, i]) for i in range(4)),
            copy(rhs.at[systems[t]], start.at[t], sems.at[t, 4]),
        ]
        for t in range(2)
    ]
    give = [copy(done.at[t], total.at[systems[t]], sems.at[t, 5]) for t in range(2)]
    take_early = [copy(factor.at[core, 1, :, cuts[i]], early.at[i], sems.at[2, i]) for i in range(2)]
    for one in (*take[0], *take[1], *take_early):
        one.start()
    for t, source in enumerate((mine, theirs)):
        for row in range(8):
            cut = slice(128 * row, 128 * row + 128)
            parts = [source[lax.rem(x - q + 4, 4), cut, :].astype(F32) for q in range(4)]
            set_blocks(blocks.at[t], 128 * row, parts)
    for t in range(2):
        for one in take[t]:
            one.wait()
        for i in range(4):
            real, imag = trail_product(rows[t, i].reshape(2 * height, 1024), blocks.at[t])
            cut = slice(i * height, i * height + height)
            done[t, 0, cut, :] = start[t, 0, cut, :].astype(F32) - real
            done[t, 1, cut, :] = start[t, 1, cut, :].astype(F32) - imag
        give[t].start()
    low = lanes_below((128, 128), 64)
    for row in range(8):
        cut = slice(128 * row, 128 * row + 128)
        real, imag = couple(blocks[0, cut, :], blocks[1, cut, :])
        before[cut, :] = jnp.where(low, real, imag)
    for one in (*take_early, *give):
        one.wait()


def trail_first(place, mine, theirs, trail_factor, trail_rhs):
    rows = trail_rhs.shape[2]
    height = rows // 4
    inside = pl.BlockSpec(memory_space=pltpu.VMEM)
    outside = pl.BlockSpec(memory_space=pltpu.HBM)
    return pl.pallas_call(
        trail_first_kernel,
        in_specs=[pl.BlockSpec(memory_space=pltpu.SMEM), inside, inside, outside, outside],
        out_specs=[outside, inside, inside],
        out_shape=[
            pltpu.HBM((2, 2, rows, 256), F32),
            pltpu.HBM((1024, 128), F32),
            pltpu.VMEM((2, 2, height, 1024), BF16),
        ],
        scratch_shapes=[
            pltpu.VMEM((2, 1024, 512), BF16),
            pltpu.VMEM((2, 4, 2, height, 1024), BF16),
            pltpu.VMEM((2, 2, rows, 256), BF16),
            pltpu.VMEM((2, 2, rows, 256), F32),
            pltpu.SemaphoreType.DMA((3, 6)),
        ],
        compiler_params=pltpu.CompilerParams(vmem_limit_bytes=28 * 1024 * 1024),
        name="trail_first",
    )(place, mine, theirs, trail_factor, trail_rhs)


def take_blocks(place, received, blocks, tiles):
    for row in range(8):
        parts = [
            received[q, :, 8 * row : 8 * row + 8, :].astype(F32).reshape(128, 128) for q in range(4)
        ]
        set_blocks(blocks, 128 * row, parts)
    for q in range(4):
        tiles[q] = received[q, :, 64:, :].astype(F32).reshape(128, 128).astype(BF16)
    near = pl.multiple_of(8 * place[2], 8)
    parts = [received[q, place[3], pl.ds(near, 8), :].astype(F32) for q in range(4)]
    pairs = [pair_lanes(parts[0], parts[1]), pair_lanes(parts[2], parts[3])]
    return [
        jnp.concatenate([pairs[0][part], pairs[1][part]], axis=1).astype(BF16) for part in range(2)
    ]


def finish_rows(i, product, before, done):
    height = done.shape[2]
    cut = slice(i * height, i * height + height)
    done[i, 0] = (before[0, cut, :] - product[0]).astype(BF16)
    done[i, 1] = (before[1, cut, :] - product[1]).astype(BF16)


def trail_mine_kernel(
    place, received, factor, early, total, out, own, blocks, tiles, later, rest, arrived, rows, before, done, sems
):
    core = place[1]
    height = rows.shape[1] // 2
    copy = pltpu.make_async_copy
    cuts = [pl.ds(i * height, height) for i in range(4)]
    take = copy(received, arrived, sems.at[0])
    take_row = copy(factor.at[core, 1, :, pl.ds(2 * height, 2 * height)], rows, sems.at[1])
    halves = [pl.ds(0, 2 * height), pl.ds(2 * height, 2 * height)]
    take_before = [
        copy(total.at[core, :, halves[i]], before.at[:, halves[i]], sems.at[(2, 12)[i]]) for i in range(2)
    ]
    take_rest = copy(total.at[1 - core], rest, sems.at[3])
    give = [copy(done.at[i], out.at[core, :, cuts[i]], sems.at[4 + i]) for i in range(4)]
    take_later = [
        copy(factor.at[1 - core, 1, :, cuts[i]], later.at[i], sems.at[8 + i]) for i in range(4)
    ]
    take.start()
    take_before[0].start()
    take.wait()
    for one in (take_row, take_before[1], *take_later, take_rest):
        one.start()
    own[0], own[1] = take_blocks(place, arrived, blocks, tiles)
    take_before[0].wait()
    for i in range(2):
        product = trail_product(early[i].reshape(2 * height, 1024), blocks)
        finish_rows(i, product, before, done)
        give[i].start()
    take_row.wait()
    take_before[1].wait()
    for i in range(2):
        cut = slice(i * height, i * height + height)
        product = trail_product(rows[:, cut, :].reshape(2 * height, 1024), blocks)
        finish_rows(2 + i, product, before, done)
        give[2 + i].start()
    for one in (*take_later, take_rest, *give):
        one.wait()


def trail_mine(place, received, trail_factor, early, total):
    rows = total.shape[2]
    height = rows // 4
    inside = pl.BlockSpec(memory_space=pltpu.VMEM)
    outside = pl.BlockSpec(memory_space=pltpu.HBM)
    return pl.pallas_call(
        trail_mine_kernel,
        in_specs=[pl.BlockSpec(memory_space=pltpu.SMEM), outside, outside, inside, outside],
        out_specs=[outside] + [inside] * 5,
        out_shape=[
            pltpu.HBM((2, 2, rows, 256), BF16),
            pltpu.VMEM((2, 8, 256), BF16),
            pltpu.VMEM((1024, 512), BF16),
            pltpu.VMEM((4, 128, 128), BF16),
            pltpu.VMEM((4, 2, height, 1024), BF16),
            pltpu.VMEM((2, rows, 256), F32),
        ],
        scratch_shapes=[
            pltpu.VMEM((4, 16, 72, 128), BF16),
            pltpu.VMEM((2, 2 * height, 1024), BF16),
            pltpu.VMEM((2, rows, 256), F32),
            pltpu.VMEM((4, 2, height, 256), BF16),
            pltpu.SemaphoreType.DMA((13,)),
        ],
        compiler_params=pltpu.CompilerParams(vmem_limit_bytes=14 * 1024 * 1024),
        name="trail_mine",
    )(place, received, trail_factor, early, total)


def trail_theirs_kernel(
    place, received, rows, rest, mine, mine_tiles, own, first, before, spread, _, out, panel, gradient, blocks, tiles, done, sems
):
    core = place[1]
    height = rows.shape[2]
    give = [
        pltpu.make_async_copy(
            done.at[i], out.at[1 - core, :, pl.ds(i * height, height)], sems.at[i]
        )
        for i in range(4)
    ]
    panel[:, 0] = first[...]
    panel[core, 1] = own[...]
    real, imag = take_blocks(place, received, blocks, tiles)
    panel[1 - core, 1, 0] = real
    panel[1 - core, 1, 1] = imag
    for i in range(4):
        product = trail_product(rows[i].reshape(2 * height, 1024), blocks)
        finish_rows(i, product, rest, done)
        give[i].start()
    slot_gradient(place, mine, blocks, (mine_tiles, tiles), before, spread, gradient)
    for one in give:
        one.wait()


def trail_theirs(place, received, later, rest, mine, mine_tiles, own, first, before, spread, update):
    height = later.shape[2]
    inside = pl.BlockSpec(memory_space=pltpu.VMEM)
    outside = pl.BlockSpec(memory_space=pltpu.HBM)
    return pl.pallas_call(
        trail_theirs_kernel,
        in_specs=[pl.BlockSpec(memory_space=pltpu.SMEM)] + [inside] * 9 + [outside],
        out_specs=[outside, inside, inside],
        out_shape=[
            pltpu.HBM(update.shape, BF16),
            jax.ShapeDtypeStruct((2, 2, 2, 8, 256), BF16),
            jax.ShapeDtypeStruct((3, 8), F32),
        ],
        scratch_shapes=[
            pltpu.VMEM((1024, 512), BF16),
            pltpu.VMEM((4, 128, 128), BF16),
            pltpu.VMEM((4, 2, height, 256), BF16),
            pltpu.SemaphoreType.DMA((4,)),
        ],
        input_output_aliases={10: 0},
        compiler_params=pltpu.CompilerParams(vmem_limit_bytes=14 * 1024 * 1024),
        name="trail_theirs",
    )(place, received, later, rest, mine, mine_tiles, own, first, before, spread, update)


def spread_matrix():
    spread = np.zeros((128, 2, 3, 128), np.float32)
    for panel in range(2):
        for corner in range(3):
            for coordinate in range(3):
                lanes = slice(24 * corner + 8 * coordinate, 24 * corner + 8 * coordinate + 8)
                for part in range(2):
                    source = 18 * part + 9 * panel + 3 * corner + coordinate
                    for term in range(3):
                        spread[36 * term + source, panel, part, lanes] = 1.0
                spread[108 + 3 * panel + corner, panel, 2, lanes] = 32.0
                spread[114 + 3 * panel + corner, panel, 2, lanes] = 1.0
    return jnp.asarray(spread.reshape(128, 768), BF16)


def couple(near, far):
    near = near.astype(F32)
    far = far.astype(F32)
    near_real, near_imag, far_real, far_imag = near[:, :256], near[:, 256:], far[:, :256], far[:, 256:]
    real = near_real * far_real - near_imag * far_imag
    imag = near_real * far_imag + near_imag * far_real
    sums = jnp.concatenate([real[:, :128] + real[:, 128:], imag[:, :128] + imag[:, 128:]])
    sums = jnp.broadcast_to(jnp.sum(sums, axis=1, keepdims=True), (256, 128))
    return sums[:128], sums[128:]


def slot_gradient(place, mine, theirs, tiles, before, spread, out):
    base = 8 * (16 * place[2] + place[3])
    target = (base + lax.rem(lax.broadcasted_iota(jnp.int32, (128, 128), 1), 8)).astype(F32)
    source_lane = lax.broadcasted_iota(jnp.int32, (128, 256), 0)
    high = lax.broadcasted_iota(jnp.int32, (128, 256), 1) >= 128
    pick = (source_lane == jnp.where(high, 64, 0)).astype(F32)
    total = jnp.zeros((8, 128), F32)
    for source in range(4):
        for side in range(2):
            row = 2 * source + (place[1] if side == 0 else 1 - place[1])
            cut = pl.ds(pl.multiple_of(128 * row, 128), 128)
            value = before[cut, :]
            first = jnp.concatenate([jnp.broadcast_to(value[:, :1], (128, 128)), jnp.broadcast_to(value[:, 64:65], (128, 128))], axis=1)
            second = couple(mine[cut, :], theirs[cut, :])
            table = jnp.dot(tiles[side][source], spread[...], preferred_element_type=F32)
            for at, real, imag in ((0, first[:, :128], first[:, 128:]), (384, *second)):
                value = table[:, at + 128 : at + 256] * imag - table[:, at : at + 128] * real
                value = jnp.where(table[:, at + 256 : at + 384] == target, value, 0.0)
                total = total + jnp.sum(value.reshape(16, 8, 128), axis=0)
    total = jnp.sum(total, axis=0, keepdims=True)
    total = total + pltpu.roll(total, 104, 1) + pltpu.roll(total, 80, 1)
    for coordinate in range(3):
        out[coordinate : coordinate + 1, :] = total[:, 8 * coordinate : 8 * coordinate + 8]


def rounds_x(value):
    sent = [lax.ppermute(value, "x", [(i, (i + step) % 4) for i in range(4)]) for step in (1, 2, 3)]
    return [value, *sent]


def swap_core(value):
    return lax.ppermute(value, "core", [(0, 1), (1, 0)])


def element_tile(shape_tiles, element_vertices, vertex_slot):
    values = shape_tiles.transpose(3, 0, 2, 1).reshape(8, 36)
    high = lax.reduce_precision(values, 8, 7)
    rest = values - high
    mid = lax.reduce_precision(rest, 8, 7)
    low = rest - mid
    slots = vertex_slot[element_vertices].transpose(1, 0, 2).reshape(8, 6)
    parts = [high, mid, low, (slots // 32).astype(F32), (slots % 32).astype(F32), jnp.zeros((8, 8), F32)]
    return jnp.concatenate(parts, axis=1).astype(BF16)


def steps(
    panel_inverse,
    panel_below,
    trail_factor,
    first_rhs,
    second_rhs,
    trail_rhs,
    shape_tiles,
    element_vertices,
    vertex_slot,
):
    x = lax.axis_index("x")
    core = lax.axis_index("core")
    col = lax.axis_index("col")
    outside = lambda value: pltpu.with_memory_space_constraint(value, pltpu.HBM)
    trail_factor, panel_inverse, first_rhs = map(outside, (trail_factor, panel_inverse, first_rhs))
    panel_below, second_rhs = map(outside, (panel_below, second_rhs))
    place = jnp.stack([x, core, 2 * x + core, col]).astype(jnp.int32)

    first, send, own, give = prepare(panel_inverse, first_rhs, panel_below, second_rhs)
    received = lax.all_to_all(send.reshape(128, 2, 8, 128), ALL, 0, 0, tiled=True)

    other = swap_core(give)
    chip = jnp.where(core == 0, jnp.stack([own, other]), jnp.stack([other, own]))
    rows = rounds_x(chip)
    tile = element_tile(shape_tiles, element_vertices, vertex_slot)

    first_block, send = right_side(place, received, rows)
    received = lax.all_to_all(send, "col", 0, 0, tiled=True)
    first_mine = rounds_x(first_block)
    first_mine = jnp.stack(first_mine)
    first_theirs = swap_core(first_mine)

    send = second_rows(place, received, rows, tile)
    second_mine = lax.all_to_all(send, ("x", "col"), 0, 0, tiled=True)

    total, before, early = trail_first(
        place, first_mine, first_theirs, trail_factor, outside(trail_rhs)
    )
    total = outside(total)

    second_theirs = swap_core(second_mine)
    mine = second_mine.reshape(4, 16, 72, 128)
    theirs = second_theirs.reshape(4, 16, 72, 128)
    update, own, mine, mine_tiles, later, rest = trail_mine(place, mine, trail_factor, early, total)
    update, panel_solution, gradient = trail_theirs(
        place,
        theirs,
        later,
        rest,
        mine,
        mine_tiles,
        own,
        first,
        before,
        spread_matrix(),
        update,
    )
    return (panel_solution, update, gradient)


def solution(mesh):
    fine = Mesh(mesh.devices.reshape(4, 2, 16), ALL)
    return jax.shard_map(
        steps,
        mesh=fine,
        in_specs=(
            P(None, None, None, ALL, None),
            P(None, None, ALL, None),
            P(None, None, None, ALL, None),
            P(),
            P(None, None, ALL, None),
            P(None, None, ALL, None),
            P(None, None, None, ALL),
            P(None, ALL, None),
            P(),
        ),
        out_specs=(
            P(None, None, None, ALL, None),
            P(None, None, ALL, None),
            P(None, ALL),
        ),
        check_vma=False,
    )
```

```python
import jax
import jax.numpy as jnp
import numpy as np
from jax import lax
from jax.experimental import pallas as pl
from jax.experimental.pallas import tpu as pltpu
from jax.sharding import Mesh
from jax.sharding import PartitionSpec as P


ALL = ("x", "core", "col")
F32 = jnp.float32
BF16 = jnp.bfloat16
SMALL_VMEM = 12 * 1024 * 1024
SPACE = pltpu.VMEM


def lanes_below(shape, bound):
    return lax.broadcasted_iota(jnp.int32, shape, len(shape) - 1) < bound


def pair_lanes(left, right):
    low = lanes_below(left.shape, 64)
    real = jnp.where(low, left, pltpu.roll(right, 64, 1))
    imag = jnp.where(low, pltpu.roll(left, 64, 1), right)
    return real, imag


def fold_parts(top, low):
    turned = pltpu.roll(low, 64, 1)
    return top + jnp.where(lanes_below(low.shape, 64), -turned, turned)


def prepare_kernel(inverse, rhs, below, own_rhs, first, send, own, give):
    system = pl.program_id(0)
    core = lax.axis_index("core")
    left = jnp.concatenate([inverse[0, 0, 0].astype(F32), inverse[0, 0, 1].astype(F32)]).astype(BF16)
    by_real = jnp.dot(left, rhs[0, 0], preferred_element_type=F32)
    by_imag = jnp.dot(left, rhs[0, 1], preferred_element_type=F32)
    real = (by_real[:8] - by_imag[8:]).astype(BF16)
    imag = (by_imag[:8] + by_real[8:]).astype(BF16)
    first[0, 0] = real
    first[0, 1] = imag
    real = real.astype(F32)
    imag = imag.astype(F32)
    for half in range(2):
        cut = slice(128 * half, 128 * half + 128)
        even, odd = pair_lanes(real[:, cut], imag[:, cut])
        for group, value in ((2 * half, even), (2 * half + 1, odd)):
            value = value.astype(BF16)
            for col in range(16):
                send[group, 0, col, 0] = value
    lane_block = lax.broadcasted_iota(jnp.int32, (8, 128), 1) // 8
    pieces = [
        below[0, part, :, 128 * row : 128 * row + 128].astype(F32)
        for part in range(2)
        for row in range(8)
    ]
    for col in range(16):
        value = pltpu.roll(pieces[0], (128 - 8 * col) % 128, 1)
        for block in range(1, 16):
            turned = pltpu.roll(pieces[block], (8 * block - 8 * col) % 128, 1)
            value = jnp.where(lane_block == block, turned, value)
        value = value.astype(BF16)
        for group in range(4):
            send[group, 0, col, 1] = value

    def fill(target):
        for part in range(2):
            target[part, :, :1024] = inverse[0, 1, part]
            target[part, :, 1024:] = own_rhs[0, part]

    @pl.when(system == core)
    def _():
        fill(own)

    @pl.when(system != core)
    def _():
        fill(give)


def prepare(panel_inverse, first_rhs, panel_below, second_rhs):
    return pl.pallas_call(
        prepare_kernel,
        grid=(2,),
        in_specs=[
            pl.BlockSpec((1, 2, 2, 8, 1024), lambda s: (s, 0, 0, 0, 0)),
            pl.BlockSpec((1, 2, 1024, 256), lambda s: (s, 0, 0, 0)),
            pl.BlockSpec((1, 2, 8, 1024), lambda s: (s, 0, 0, 0)),
            pl.BlockSpec((1, 2, 8, 256), lambda s: (s, 0, 0, 0)),
        ],
        out_specs=[
            pl.BlockSpec((1, 2, 8, 256), lambda s: (s, 0, 0, 0)),
            pl.BlockSpec((4, 1, 16, 2, 8, 128), lambda s: (0, s, 0, 0, 0, 0)),
            pl.BlockSpec((2, 8, 1280), lambda s: (0, 0, 0)),
            pl.BlockSpec((2, 8, 1280), lambda s: (0, 0, 0)),
        ],
        out_shape=[
            jax.ShapeDtypeStruct((2, 2, 8, 256), BF16),
            jax.ShapeDtypeStruct((4, 2, 16, 2, 8, 128), BF16),
            jax.ShapeDtypeStruct((2, 8, 1280), BF16),
            jax.ShapeDtypeStruct((2, 8, 1280), BF16),
        ],
        compiler_params=pltpu.CompilerParams(vmem_limit_bytes=SMALL_VMEM),
        name="prepare",
    )(panel_inverse, first_rhs, panel_below, second_rhs)


def right_kernel(place, received, rows0, rows1, rows2, rows3, block, send, offset):
    x = place[0]
    half = pl.multiple_of(1024 + 128 * (x // 2), 128)
    odd = x % 2 == 1
    for step, rows in enumerate((rows0, rows1, rows2, rows3)):
        source = lax.rem(x - step + 4, 4)
        for core in range(2):
            real = rows[core, 0, :, pl.ds(half, 128)].astype(F32)
            imag = rows[core, 1, :, pl.ds(half, 128)].astype(F32)
            even_pair, odd_pair = pair_lanes(real, imag)
            value = jnp.where(odd, odd_pair, even_pair)
            offset[pl.ds(pl.multiple_of(16 * source + 8 * core, 8), 8), :] = value
    first = received[:, 0].astype(F32).reshape(1024, 128).astype(BF16)
    below = received[:, 1].astype(F32).reshape(1024, 128).astype(BF16)
    block[...] = first
    product = lax.dot_general(below, first, (((0,), (0,)), ((), ())), preferred_element_type=F32)
    right = (offset[...] - fold_parts(product[:64], product[64:])).astype(BF16)
    for col in range(16):
        send[col] = right


def right_side(place, received, rows):
    inside = pl.BlockSpec(memory_space=pltpu.VMEM)
    return pl.pallas_call(
        right_kernel,
        in_specs=[pl.BlockSpec(memory_space=pltpu.SMEM)] + [inside] * 5,
        out_specs=[inside] * 2,
        out_shape=[SPACE((1024, 128), BF16), SPACE((16, 64, 128), BF16)],
        scratch_shapes=[pltpu.VMEM((64, 128), F32)],
        compiler_params=pltpu.CompilerParams(vmem_limit_bytes=SMALL_VMEM),
        name="right_side",
    )(place, received, *rows)


def second_kernel(place, received, rows0, rows1, rows2, rows3, tile, send):
    x = place[0]
    right = received[...].astype(F32).reshape(16, 8, 8, 128)
    right = right.transpose(1, 0, 2, 3).reshape(1024, 128).astype(BF16)
    pieces = [
        rows[core, part, :, :1024].astype(F32)
        for part in range(2)
        for rows in (rows0, rows1, rows2, rows3)
        for core in range(2)
    ]
    left = jnp.concatenate(pieces).astype(BF16)
    product = jnp.dot(left, right, preferred_element_type=F32)
    value = fold_parts(product[:64], product[64:]).astype(BF16)
    for step in range(4):
        target = pl.multiple_of(16 * lax.rem(x - step + 4, 4), 16)
        part = value[16 * step : 16 * step + 16]
        for copy in range(64):
            send[copy, pl.ds(target, 16), :] = part
    for copy in range(64):
        send[copy, 64:] = tile[...]


def second_rows(place, received, rows, tile):
    inside = pl.BlockSpec(memory_space=pltpu.VMEM)
    return pl.pallas_call(
        second_kernel,
        in_specs=[pl.BlockSpec(memory_space=pltpu.SMEM)] + [inside] * 6,
        out_specs=inside,
        out_shape=SPACE((64, 72, 128), BF16),
        compiler_params=pltpu.CompilerParams(vmem_limit_bytes=SMALL_VMEM),
        name="second_rows",
    )(place, received, *rows, tile)


def set_blocks(blocks, at, parts):
    for half in range(2):
        real, imag = pair_lanes(parts[2 * half], parts[2 * half + 1])
        blocks[at : at + 128, 128 * half : 128 * half + 128] = real.astype(BF16)
        blocks[at : at + 128, 256 + 128 * half : 384 + 128 * half] = imag.astype(BF16)


def trail_product(stacked, blocks):
    height = stacked.shape[0] // 2
    product = jnp.dot(stacked, blocks[...], preferred_element_type=F32)
    top, low = product[:height], product[height:]
    return top[:, :256] - low[:, 256:], top[:, 256:] + low[:, :256]


def trail_first_kernel(place, mine, theirs, factor, rhs, total, before, early, blocks, rows, start, done, sems):
    x, core = place[0], place[1]
    height = rows.shape[3]
    copy = pltpu.make_async_copy
    cuts = [pl.ds(i * height, height) for i in range(4)]
    systems = (core, 1 - core)
    take = [
        [
            *(copy(factor.at[systems[t], 0, :, cuts[i]], rows.at[t, i], sems.at[t, i]) for i in range(4)),
            copy(rhs.at[systems[t]], start.at[t], sems.at[t, 4]),
        ]
        for t in range(2)
    ]
    give = [copy(done.at[t], total.at[systems[t]], sems.at[t, 5]) for t in range(2)]
    take_early = [copy(factor.at[core, 1, :, cuts[i]], early.at[i], sems.at[2, i]) for i in range(2)]
    for one in (*take[0], *take[1], *take_early):
        one.start()
    for t, source in enumerate((mine, theirs)):
        for row in range(8):
            cut = slice(128 * row, 128 * row + 128)
            parts = [source[lax.rem(x - q + 4, 4), cut, :].astype(F32) for q in range(4)]
            set_blocks(blocks.at[t], 128 * row, parts)
    for t in range(2):
        for one in take[t]:
            one.wait()
        for i in range(4):
            real, imag = trail_product(rows[t, i].reshape(2 * height, 1024), blocks.at[t])
            cut = slice(i * height, i * height + height)
            done[t, 0, cut, :] = start[t, 0, cut, :].astype(F32) - real
            done[t, 1, cut, :] = start[t, 1, cut, :].astype(F32) - imag
        give[t].start()
    low = lanes_below((128, 128), 64)
    for row in range(8):
        cut = slice(128 * row, 128 * row + 128)
        real, imag = couple(blocks[0, cut, :], blocks[1, cut, :])
        before[cut, :] = jnp.where(low, real, imag)
    for one in (*take_early, *give):
        one.wait()


def trail_first(place, mine, theirs, trail_factor, trail_rhs):
    rows = trail_rhs.shape[2]
    height = rows // 4
    inside = pl.BlockSpec(memory_space=pltpu.VMEM)
    outside = pl.BlockSpec(memory_space=pltpu.HBM)
    return pl.pallas_call(
        trail_first_kernel,
        in_specs=[pl.BlockSpec(memory_space=pltpu.SMEM), inside, inside, outside, outside],
        out_specs=[outside, inside, inside],
        out_shape=[
            pltpu.HBM((2, 2, rows, 256), F32),
            pltpu.HBM((1024, 128), F32),
            pltpu.VMEM((2, 2, height, 1024), BF16),
        ],
        scratch_shapes=[
            pltpu.VMEM((2, 1024, 512), BF16),
            pltpu.VMEM((2, 4, 2, height, 1024), BF16),
            pltpu.VMEM((2, 2, rows, 256), BF16),
            pltpu.VMEM((2, 2, rows, 256), F32),
            pltpu.SemaphoreType.DMA((3, 6)),
        ],
        compiler_params=pltpu.CompilerParams(vmem_limit_bytes=28 * 1024 * 1024),
        name="trail_first",
    )(place, mine, theirs, trail_factor, trail_rhs)


def take_blocks(place, received, blocks, tiles):
    for row in range(8):
        parts = [
            received[q, :, 8 * row : 8 * row + 8, :].astype(F32).reshape(128, 128) for q in range(4)
        ]
        set_blocks(blocks, 128 * row, parts)
    for q in range(4):
        tiles[q] = received[q, :, 64:, :].astype(F32).reshape(128, 128).astype(BF16)
    near = pl.multiple_of(8 * place[2], 8)
    parts = [received[q, place[3], pl.ds(near, 8), :].astype(F32) for q in range(4)]
    pairs = [pair_lanes(parts[0], parts[1]), pair_lanes(parts[2], parts[3])]
    return [
        jnp.concatenate([pairs[0][part], pairs[1][part]], axis=1).astype(BF16) for part in range(2)
    ]


def finish_rows(i, product, before, done):
    height = done.shape[2]
    cut = slice(i * height, i * height + height)
    done[i, 0] = (before[0, cut, :] - product[0]).astype(BF16)
    done[i, 1] = (before[1, cut, :] - product[1]).astype(BF16)


def trail_mine_kernel(
    place, received, factor, early, total, out, own, blocks, tiles, later, rest, rows, before, done, sems
):
    core = place[1]
    height = rows.shape[1] // 2
    copy = pltpu.make_async_copy
    cuts = [pl.ds(i * height, height) for i in range(4)]
    take_row = copy(factor.at[core, 1, :, pl.ds(2 * height, 2 * height)], rows, sems.at[1])
    halves = [pl.ds(0, 2 * height), pl.ds(2 * height, 2 * height)]
    take_before = [
        copy(total.at[core, :, halves[i]], before.at[:, halves[i]], sems.at[(2, 12)[i]]) for i in range(2)
    ]
    take_rest = copy(total.at[1 - core], rest, sems.at[3])
    give = [copy(done.at[i], out.at[core, :, cuts[i]], sems.at[4 + i]) for i in range(4)]
    take_later = [
        copy(factor.at[1 - core, 1, :, cuts[i]], later.at[i], sems.at[8 + i]) for i in range(4)
    ]
    take_before[0].start()
    for one in (take_row, take_before[1], *take_later, take_rest):
        one.start()
    own[0], own[1] = take_blocks(place, received, blocks, tiles)
    take_before[0].wait()
    for i in range(2):
        product = trail_product(early[i].reshape(2 * height, 1024), blocks)
        finish_rows(i, product, before, done)
        give[i].start()
    take_row.wait()
    take_before[1].wait()
    for i in range(2):
        cut = slice(i * height, i * height + height)
        product = trail_product(rows[:, cut, :].reshape(2 * height, 1024), blocks)
        finish_rows(2 + i, product, before, done)
        give[2 + i].start()
    for one in (*take_later, take_rest, *give):
        one.wait()


def trail_mine(place, received, trail_factor, early, total):
    rows = total.shape[2]
    height = rows // 4
    inside = pl.BlockSpec(memory_space=pltpu.VMEM)
    outside = pl.BlockSpec(memory_space=pltpu.HBM)
    return pl.pallas_call(
        trail_mine_kernel,
        in_specs=[pl.BlockSpec(memory_space=pltpu.SMEM), inside, outside, inside, outside],
        out_specs=[outside] + [inside] * 5,
        out_shape=[
            pltpu.HBM((2, 2, rows, 256), BF16),
            pltpu.VMEM((2, 8, 256), BF16),
            pltpu.VMEM((1024, 512), BF16),
            pltpu.VMEM((4, 128, 128), BF16),
            pltpu.VMEM((4, 2, height, 1024), BF16),
            pltpu.VMEM((2, rows, 256), F32),
        ],
        scratch_shapes=[
            pltpu.VMEM((2, 2 * height, 1024), BF16),
            pltpu.VMEM((2, rows, 256), F32),
            pltpu.VMEM((4, 2, height, 256), BF16),
            pltpu.SemaphoreType.DMA((13,)),
        ],
        compiler_params=pltpu.CompilerParams(vmem_limit_bytes=14 * 1024 * 1024),
        name="trail_mine",
    )(place, received, trail_factor, early, total)


def trail_theirs_kernel(
    place, received, rows, rest, mine, mine_tiles, own, first, before, spread, _, out, panel, gradient, blocks, tiles, done, sems
):
    core = place[1]
    height = rows.shape[2]
    give = [
        pltpu.make_async_copy(
            done.at[i], out.at[1 - core, :, pl.ds(i * height, height)], sems.at[i]
        )
        for i in range(4)
    ]
    panel[:, 0] = first[...]
    panel[core, 1] = own[...]
    real, imag = take_blocks(place, received, blocks, tiles)
    panel[1 - core, 1, 0] = real
    panel[1 - core, 1, 1] = imag
    for i in range(4):
        product = trail_product(rows[i].reshape(2 * height, 1024), blocks)
        finish_rows(i, product, rest, done)
        give[i].start()
    slot_gradient(place, mine, blocks, (mine_tiles, tiles), before, spread, gradient)
    for one in give:
        one.wait()


def trail_theirs(place, received, later, rest, mine, mine_tiles, own, first, before, spread, update):
    height = later.shape[2]
    inside = pl.BlockSpec(memory_space=pltpu.VMEM)
    outside = pl.BlockSpec(memory_space=pltpu.HBM)
    return pl.pallas_call(
        trail_theirs_kernel,
        in_specs=[pl.BlockSpec(memory_space=pltpu.SMEM)] + [inside] * 9 + [outside],
        out_specs=[outside, inside, inside],
        out_shape=[
            pltpu.HBM(update.shape, BF16),
            jax.ShapeDtypeStruct((2, 2, 2, 8, 256), BF16),
            jax.ShapeDtypeStruct((3, 8), F32),
        ],
        scratch_shapes=[
            pltpu.VMEM((1024, 512), BF16),
            pltpu.VMEM((4, 128, 128), BF16),
            pltpu.VMEM((4, 2, height, 256), BF16),
            pltpu.SemaphoreType.DMA((4,)),
        ],
        input_output_aliases={10: 0},
        compiler_params=pltpu.CompilerParams(vmem_limit_bytes=14 * 1024 * 1024),
        name="trail_theirs",
    )(place, received, later, rest, mine, mine_tiles, own, first, before, spread, update)


def spread_matrix():
    spread = np.zeros((128, 2, 3, 128), np.float32)
    for panel in range(2):
        for corner in range(3):
            for coordinate in range(3):
                lanes = slice(24 * corner + 8 * coordinate, 24 * corner + 8 * coordinate + 8)
                for part in range(2):
                    source = 18 * part + 9 * panel + 3 * corner + coordinate
                    for term in range(3):
                        spread[36 * term + source, panel, part, lanes] = 1.0
                spread[108 + 3 * panel + corner, panel, 2, lanes] = 32.0
                spread[114 + 3 * panel + corner, panel, 2, lanes] = 1.0
    return jnp.asarray(spread.reshape(128, 768), BF16)


def couple(near, far):
    near = near.astype(F32)
    far = far.astype(F32)
    near_real, near_imag, far_real, far_imag = near[:, :256], near[:, 256:], far[:, :256], far[:, 256:]
    real = near_real * far_real - near_imag * far_imag
    imag = near_real * far_imag + near_imag * far_real
    sums = jnp.concatenate([real[:, :128] + real[:, 128:], imag[:, :128] + imag[:, 128:]])
    sums = jnp.broadcast_to(jnp.sum(sums, axis=1, keepdims=True), (256, 128))
    return sums[:128], sums[128:]


def slot_gradient(place, mine, theirs, tiles, before, spread, out):
    base = 8 * (16 * place[2] + place[3])
    target = (base + lax.rem(lax.broadcasted_iota(jnp.int32, (128, 128), 1), 8)).astype(F32)
    source_lane = lax.broadcasted_iota(jnp.int32, (128, 256), 0)
    high = lax.broadcasted_iota(jnp.int32, (128, 256), 1) >= 128
    pick = (source_lane == jnp.where(high, 64, 0)).astype(F32)
    total = jnp.zeros((8, 128), F32)
    for source in range(4):
        for side in range(2):
            row = 2 * source + (place[1] if side == 0 else 1 - place[1])
            cut = pl.ds(pl.multiple_of(128 * row, 128), 128)
            value = before[cut, :]
            first = jnp.concatenate([jnp.broadcast_to(value[:, :1], (128, 128)), jnp.broadcast_to(value[:, 64:65], (128, 128))], axis=1)
            second = couple(mine[cut, :], theirs[cut, :])
            table = jnp.dot(tiles[side][source], spread[...], preferred_element_type=F32)
            for at, real, imag in ((0, first[:, :128], first[:, 128:]), (384, *second)):
                value = table[:, at + 128 : at + 256] * imag - table[:, at : at + 128] * real
                value = jnp.where(table[:, at + 256 : at + 384] == target, value, 0.0)
                total = total + jnp.sum(value.reshape(16, 8, 128), axis=0)
    total = jnp.sum(total, axis=0, keepdims=True)
    total = total + pltpu.roll(total, 104, 1) + pltpu.roll(total, 80, 1)
    for coordinate in range(3):
        out[coordinate : coordinate + 1, :] = total[:, 8 * coordinate : 8 * coordinate + 8]


def rounds_x(value):
    sent = [lax.ppermute(value, "x", [(i, (i + step) % 4) for i in range(4)]) for step in (1, 2, 3)]
    return [value, *sent]


def swap_core(value):
    return lax.ppermute(value, "core", [(0, 1), (1, 0)])


def element_tile(shape_tiles, element_vertices, vertex_slot):
    values = shape_tiles.transpose(3, 0, 2, 1).reshape(8, 36)
    high = lax.reduce_precision(values, 8, 7)
    rest = values - high
    mid = lax.reduce_precision(rest, 8, 7)
    low = rest - mid
    slots = vertex_slot[element_vertices].transpose(1, 0, 2).reshape(8, 6)
    parts = [high, mid, low, (slots // 32).astype(F32), (slots % 32).astype(F32), jnp.zeros((8, 8), F32)]
    return jnp.concatenate(parts, axis=1).astype(BF16)


def steps(
    panel_inverse,
    panel_below,
    trail_factor,
    first_rhs,
    second_rhs,
    trail_rhs,
    shape_tiles,
    element_vertices,
    vertex_slot,
):
    x = lax.axis_index("x")
    core = lax.axis_index("core")
    col = lax.axis_index("col")
    outside = lambda value: pltpu.with_memory_space_constraint(value, pltpu.HBM)
    trail_factor, panel_inverse, first_rhs = map(outside, (trail_factor, panel_inverse, first_rhs))
    panel_below, second_rhs = map(outside, (panel_below, second_rhs))
    place = jnp.stack([x, core, 2 * x + core, col]).astype(jnp.int32)

    first, send, own, give = prepare(panel_inverse, first_rhs, panel_below, second_rhs)
    received = lax.all_to_all(send.reshape(128, 2, 8, 128), ALL, 0, 0, tiled=True)

    other = swap_core(give)
    chip = jnp.where(core == 0, jnp.stack([own, other]), jnp.stack([other, own]))
    rows = rounds_x(chip)
    tile = element_tile(shape_tiles, element_vertices, vertex_slot)

    first_block, send = right_side(place, received, rows)
    received = lax.all_to_all(send, "col", 0, 0, tiled=True)
    first_mine = rounds_x(first_block)
    first_mine = jnp.stack(first_mine)
    first_theirs = swap_core(first_mine)

    send = second_rows(place, received, rows, tile)
    second_mine = lax.all_to_all(send, ("x", "col"), 0, 0, tiled=True)

    total, before, early = trail_first(
        place, first_mine, first_theirs, trail_factor, outside(trail_rhs)
    )
    total = outside(total)

    second_theirs = swap_core(second_mine)
    mine = second_mine.reshape(4, 16, 72, 128)
    theirs = second_theirs.reshape(4, 16, 72, 128)
    update, own, mine, mine_tiles, later, rest = trail_mine(place, mine, trail_factor, early, total)
    update, panel_solution, gradient = trail_theirs(
        place,
        theirs,
        later,
        rest,
        mine,
        mine_tiles,
        own,
        first,
        before,
        spread_matrix(),
        update,
    )
    return (panel_solution, update, gradient)


def solution(mesh):
    fine = Mesh(mesh.devices.reshape(4, 2, 16), ALL)
    return jax.shard_map(
        steps,
        mesh=fine,
        in_specs=(
            P(None, None, None, ALL, None),
            P(None, None, ALL, None),
            P(None, None, None, ALL, None),
            P(),
            P(None, None, ALL, None),
            P(None, None, ALL, None),
            P(None, None, None, ALL),
            P(None, ALL, None),
            P(),
        ),
        out_specs=(
            P(None, None, None, ALL, None),
            P(None, None, ALL, None),
            P(None, ALL),
        ),
        check_vma=False,
    )
```
